256 devices in a mesh: expert: 128 (over y, z, x), half: 2 (over core).
Axes of the slice: x: 4, y: 4, z: 8, core: 2. Of those that a mesh axis runs over, the one named last changes fastest.
Arguments:
- tokens: bfloat16 [8192, 2048], P('expert'), may hold values from -6 to 6
- cotangent: bfloat16 [8192, 2048], P('expert'), may hold values from -1 to 1
- expert_ids: int32 [8192, 8], P('expert'), may hold values from 0 to 127, all different within a row; in each aligned block of 64 rows (0 to 63, 64 to 127, ...) at most 6 rows name the same one
- gate_weights: float32 [8192, 8], P('expert'), may hold values from 0.1 to 0.6
- w_gate: bfloat16 [128, 2048, 768], P('expert', None, 'half'), may hold values from -0.125 to 0.125
- w_up: bfloat16 [128, 2048, 768], P('expert', None, 'half'), may hold values from -0.125 to 0.125
- w_down: bfloat16 [128, 768, 2048], P('expert', 'half'), may hold values from -0.21875 to 0.21875
Outputs:
- input_grad: bfloat16 [8192, 2048], P('expert')
- gate_grad: bfloat16 [8192, 8], P('expert')
The draws below stay inside these ranges and needn't reach their ends.
Inputs may be any that keep to these rules, and one draw needn't show every extreme that they name: `expert_ids`: each token names 8 different experts. Among the 64 tokens of one index of expert, no expert is named by more than 6 tokens, a bound that some block reaches; every expert is named somewhere.
All inputs are finite; a program needn't handle non-finite values.
Results may differ from the reference program's by a relative error of at most 0.0085.
Values may be sent and summed in bfloat16 or wider, within the bound.
A program may use at most 64 MiB of HBM per device.

```python
import math
import jax
import jax.numpy as jnp
import numpy as np
from jax import lax

D = 2048
FF = 768
TOP = 8
TOK_DEV = 64
EXPERTS = 128
CAP = 6
TOKENS = 8192
N_EXPERT = 128


def level_of(rng, extent, cuts, smallest, high):
    def one(dim, parts):
        steps = jax.random.uniform(jax.random.fold_in(jax.random.fold_in(rng, 6), dim), (parts,), jnp.float32, smallest / len(cuts), high / len(cuts))
        return jnp.repeat(jnp.exp(steps), extent[dim] // parts).reshape((-1,) + (1,) * (len(extent) - dim - 1))

    factor_of = one(*cuts[0])
    for cut in cuts[1:]:
        factor_of = factor_of * one(*cut)
    return factor_of


def routed_block(stream_key, own, number, rows, number_of, top, most, lean):
    sequence = jax.random.permutation(stream_key, number_of)
    packed, ordinary = portions_of(number_of, rows * top, most, lean, True), portions_of(number_of, rows * top, most, lean, False)
    places = jnp.arange(number_of)

    def named(sizes, offset_by):
        used = int((sizes > 0).sum())
        fixed = max(1, used // 4)
        passed = fixed + (places - fixed + offset_by * (used - fixed)) % max(1, number_of - fixed)
        return jnp.zeros((number_of,), jnp.int32).at[sequence[jnp.where(places < fixed, places, passed)]].set(jnp.asarray(sizes, jnp.int32))

    sizes = jnp.where(number % 4 == 0, named(packed, number // 4), named(ordinary, number - number // 4 - 1))
    mixed = jax.random.permutation(jax.random.fold_in(own, 3), number_of)
    donor, receiver = mixed[0:number_of // 2 * 2:2], mixed[1:number_of // 2 * 2:2]
    margin = jnp.minimum(sizes[donor] - 1, most - sizes[receiver]) // 2
    margin = jnp.where((donor == sequence[0]) | (receiver == sequence[0]) | (sizes[receiver] == 0), 0, jnp.maximum(margin, 0))
    passed = jax.random.randint(jax.random.fold_in(own, 4), (number_of // 2,), 0, 1 << 20) % (margin + 1)
    sizes = sizes.at[donor].add(-passed).at[receiver].add(passed)
    items = jnp.searchsorted(jnp.cumsum(sizes), jnp.arange(rows * top), side="right").astype(jnp.int32)
    listing = items.reshape(top, rows).T
    listing = listing[jax.random.permutation(jax.random.fold_in(own, 1), rows)]
    offset_by = jax.random.randint(jax.random.fold_in(own, 2), (rows, 1), 0, top)
    return jnp.take_along_axis(listing, (jnp.arange(top)[None, :] + offset_by) % top, axis=1)


def portions_of(amount, total, bound, lean, full):
    loads = [(1 << 20) // math.isqrt(standing ** lean) + 1 for standing in range(1, amount + 1)]
    largest = bound if full else min(bound, max(-(-total // amount), total * loads[0] // sum(loads)))
    least = 1 if total - largest >= amount - 1 else 0
    holding, rest = [largest] + [least] * (amount - 1), total - largest - least * (amount - 1)
    while rest > 0:
        candidates = [i for i in range(1, amount) if holding[i] < largest] or [i for i in range(1, amount) if holding[i] < bound]
        pool, remaining = sum([loads[i] for i in candidates]), rest
        for i in candidates:
            addition = min(bound - holding[i], max(1, remaining * loads[i] // pool), rest)
            holding[i] = holding[i] + addition
            rest = rest - addition
    return np.array(holding)


def scatter_about(own_key, extent, scale, bound, split=(), kind=jnp.bfloat16):
    factor_of = level_of(own_key, extent, split, -0.22, 0.18) if split else 1.0
    array = jax.random.normal(own_key, extent, jnp.float32) * scale * factor_of
    return jnp.minimum(jnp.maximum(array, -bound), bound).astype(kind)


def setup_inputs(seed: int = 0) -> dict:
    keys = jax.random.split(jax.random.key(seed), 8)
    tokens = scatter_about(keys[0], (TOKENS, D), 1.0, 6.0, ((0, 128),))
    cotangent = scatter_about(keys[1], (TOKENS, D), 0.15, 1.0, ((0, 128),))
    expert_ids_keys = jax.random.split(jax.random.fold_in(keys[2], 1), TOKENS // TOK_DEV)
    expert_ids_turns = jax.random.permutation(jax.random.fold_in(keys[2], 3), TOKENS // TOK_DEV)
    expert_ids = jax.vmap(lambda own, number: routed_block(jax.random.fold_in(keys[2], 2), own, number, TOK_DEV, EXPERTS, TOP, CAP, 2))(expert_ids_keys, expert_ids_turns).reshape((TOKENS, TOP))
    gate_weights = jnp.clip(0.1 + 0.5 * jax.random.uniform(keys[3], (TOKENS, TOP), jnp.float32) ** level_of(keys[3], (TOKENS, TOP), ((0, 128),), -0.2, 0.2), 0.1, 0.6)
    w_gate = scatter_about(keys[4], (EXPERTS, D, FF), D ** -0.5, 0.125, ((0, 128), (2, 2)))
    w_up = scatter_about(keys[5], (EXPERTS, D, FF), D ** -0.5, 0.125, ((0, 128), (2, 2)))
    w_down = scatter_about(keys[6], (EXPERTS, FF, D), FF ** -0.5, 0.21875, ((0, 128), (1, 2)))
    return dict(tokens=tokens, cotangent=cotangent, expert_ids=expert_ids, gate_weights=gate_weights, w_gate=w_gate, w_up=w_up, w_down=w_down)


def expert_terms(rows, grads, gate_one, up_one, down_one):
    gate_pre = jnp.dot(rows, gate_one, preferred_element_type=jnp.float32)
    up_pre = jnp.dot(rows, up_one, preferred_element_type=jnp.float32)
    grad_hidden = jnp.dot(grads, down_one.T, preferred_element_type=jnp.float32)
    sigmoid_gate = jax.nn.sigmoid(gate_pre)
    silu_gate = gate_pre * sigmoid_gate
    scores = jnp.sum(grad_hidden * silu_gate * up_pre, axis=-1)
    grad_up = (grad_hidden * silu_gate).astype(jnp.bfloat16)
    grad_gate = (grad_hidden * up_pre * sigmoid_gate * (1.0 + gate_pre * (1.0 - sigmoid_gate))).astype(jnp.bfloat16)
    input_part = jnp.dot(grad_gate, gate_one.T, preferred_element_type=jnp.float32)
    input_part = input_part + jnp.dot(grad_up, up_one.T, preferred_element_type=jnp.float32)
    return input_part, scores


def reference(tokens, cotangent, expert_ids, gate_weights, w_gate, w_up, w_down):
    tok_total = tokens.shape[0]
    routed = expert_ids.reshape(-1).astype(jnp.int32)
    pair_total = routed.shape[0]
    order = jnp.argsort(routed, stable=True).astype(jnp.int32)
    counts = jnp.bincount(routed, length=EXPERTS).astype(jnp.int32)
    starts = (jnp.cumsum(counts) - counts).astype(jnp.int32)
    most = N_EXPERT * CAP
    gates_flat = gate_weights.reshape(-1)

    def visit(totals, expert):
        input_sum, gate_sum = totals
        offsets = jnp.arange(most, dtype=jnp.int32)
        slot_live = offsets < counts[expert]
        pairs = order[jnp.minimum(starts[expert] + offsets, pair_total - 1)].astype(jnp.int32)
        owners = (pairs // TOP).astype(jnp.int32)
        rows = jnp.where(slot_live[:, None], tokens[owners], jnp.zeros((), tokens.dtype))
        grads = jnp.where(slot_live[:, None], cotangent[owners], jnp.zeros((), cotangent.dtype))
        input_part, scores = expert_terms(rows, grads, w_gate[expert], w_up[expert], w_down[expert])
        rounded = lax.optimization_barrier(input_part.astype(jnp.bfloat16)).astype(jnp.float32)
        weighted = jnp.where(slot_live[:, None], gates_flat[pairs][:, None] * rounded, jnp.zeros((), jnp.float32))
        input_sum = input_sum.at[owners].add(weighted)
        gate_sum = gate_sum.at[pairs].add(jnp.where(slot_live, scores, jnp.zeros((), jnp.float32)))
        return (input_sum, gate_sum), None

    start_state = (jnp.zeros((tok_total, D), jnp.float32), jnp.zeros((pair_total,), jnp.float32))
    (input_sum, gate_sum), unused = lax.scan(visit, start_state, jnp.arange(EXPERTS, dtype=jnp.int32))
    return input_sum.astype(jnp.bfloat16), gate_sum.reshape(tok_total, TOP).astype(jnp.bfloat16)
```

```python
import functools

import jax
import jax.numpy as jnp
from jax import lax
from jax.experimental import pallas as pl
from jax.experimental.pallas import tpu as pltpu
from jax.sharding import PartitionSpec as P

MESH = pl.DeviceIdType.MESH
F32 = jnp.float32
BF16 = jnp.bfloat16
NY, NZ, NX = 4, 8, 4
CAP = 6
LANES = 128


def nt(a, b):
    return lax.dot_general(a, b, (((1,), (1,)), ((), ())), preferred_element_type=F32)


def nn(a, b):
    return jnp.dot(a, b, preferred_element_type=F32)


class Sizes:
    def __init__(self, tok, dim, half_ff, top, ny, nz, nx, chunks):
        self.tok, self.dim, self.hf, self.ff, self.top = tok, dim, half_ff, 2 * half_ff, top
        self.ny, self.nz, self.nx, self.nq = ny, nz, nx, chunks
        self.xy = ny * nx
        self.src = self.xy // 2
        self.slots = CAP * nz
        self.dc = dim // chunks
        self.rows = self.src * self.slots
        self.all_slots = self.xy * self.slots
        self.col = nz * tok
        self.dh = dim // 2
        self.rc = self.dh // 2


def kernel(
    g, raw_ref, ids_ref, tok_hbm, cot_hbm, wg_hbm, wu_hbm, wd_hbm, out_ref, gate_ref,
    xall, rawall, pick, scaled, pick_t, scaled_t, sbuf, rbuf, wg, wu, wd, gacc, uacc, hacc, gg, gu,
    ret0, ret1, back0, back1, part0, part1, rsend0, rsend1, rrecv0, rrecv1,
    own_sem, w_own_sem, w_send, w_recv, raw_send, raw_recv, z_send, z_recv, xy_send, xy_recv,
    ret_send, ret_recv, rs_send, rs_recv, out_send, out_recv,
):
    e = lax.axis_index("expert")
    c = lax.axis_index("half")
    x = lax.rem(e, g.nx)
    z = lax.rem(e // g.nx, g.nz)
    y = e // (g.nx * g.nz)
    other = 1 - c
    parity = lax.rem(x + y, 2)

    def chip(yy, zz, xx):
        return (yy * g.nz + zz) * g.nx + xx

    def zmod(v):
        return lax.rem(v + 2 * g.nz, g.nz)

    def own_copy(q, src):
        return pltpu.make_async_copy(src.at[:, pl.ds(q * g.dc, g.dc)], xall.at[q, z], own_sem.at[q])

    for q in range(g.nq):
        @pl.when(c == 0)
        def _():
            own_copy(q, tok_hbm).start()

        @pl.when(c == 1)
        def _():
            own_copy(q, cot_hbm).start()

    cut = pl.ds(pl.multiple_of(c * g.hf, LANES), g.hf)
    places = (wg.at[:, cut], wu.at[:, cut], wd.at[cut, :])
    weights = (wg_hbm.at[0], wu_hbm.at[0], wd_hbm.at[0])

    def weight_own(i):
        return pltpu.make_async_copy(weights[i], places[i], w_own_sem.at[i])

    def weight_swap(i):
        return pltpu.make_async_remote_copy(
            places[i], places[i], w_send.at[i], w_recv.at[i], device_id=(e, other), device_id_type=MESH
        )

    for i in range(3):
        weight_own(i).start()
    rawall[z] = raw_ref[...]

    barrier = pltpu.get_barrier_semaphore()
    for dy in range(g.ny):
        for dx in range(g.nx):
            peer = chip(lax.rem(y + dy, g.ny), z, lax.rem(x + dx, g.nx))
            if dy or dx:
                pl.semaphore_signal(barrier, inc=1, device_id=(peer, c), device_id_type=MESH)
            pl.semaphore_signal(barrier, inc=1, device_id=(peer, other), device_id_type=MESH)
    for dz in range(1, g.nz):
        pl.semaphore_signal(barrier, inc=1, device_id=(chip(y, zmod(z + dz), x), c), device_id_type=MESH)
    pl.semaphore_wait(barrier, 2 * g.xy - 1 + g.nz - 1)

    def raw_copy(dz):
        return pltpu.make_async_remote_copy(
            rawall.at[z], rawall.at[z], raw_send.at[dz - 1], raw_recv.at[dz - 1],
            device_id=(chip(y, zmod(z + dz), x), c), device_id_type=MESH,
        )

    for dz in range(1, g.nz):
        raw_copy(dz).start()

    def hops(q, way):
        return g.nz // 2 if (q + way) % 2 == 0 else g.nz // 2 - 1

    def z_copy(q, way, step):
        sign = 1 - 2 * way
        block = zmod(z - sign * (step - 1))
        return pltpu.make_async_remote_copy(
            xall.at[q, block], xall.at[q, block], z_send.at[q, way, step - 1], z_recv.at[q, way, step - 1],
            device_id=(chip(y, zmod(z + sign), x), c), device_id_type=MESH,
        )

    for q in range(g.nq):
        own_copy(q, tok_hbm).wait()
    for q in range(2):
        for way in range(2):
            z_copy(q, way, 1).start()
    for i in range(3):
        weight_own(i).wait()
        weight_swap(i).start()

    for dz in range(1, g.nz):
        raw_copy(dz).wait_recv()
    lane = lax.broadcasted_iota(jnp.int32, (16, LANES), 1)
    pairs = [
        jnp.where(lane < g.tok, rawall[2 * p], rawall[2 * p + 1]) for p in range(g.nz // 2)
    ]
    raw = jnp.concatenate(pairs, axis=1)
    place = lax.broadcasted_iota(jnp.int32, (g.xy, g.col), 0)
    named_by = (((place // g.nx) * g.nz + z) * g.nx + lax.rem(place, g.nx)).astype(F32)
    named = jnp.zeros((g.xy, g.col), F32)
    weight = jnp.zeros((g.xy, g.col), F32)
    for k in range(g.top):
        hit = raw[k:k + 1, :] == named_by
        named = named + jnp.where(hit, 1.0, 0.0)
        weight = weight + jnp.where(hit, raw[8 + k:9 + k, :], 0.0)
    early = lax.broadcasted_iota(jnp.int32, (g.col, g.col), 0)
    late = lax.broadcasted_iota(jnp.int32, (g.col, g.col), 1)
    before = jnp.where((early // g.tok == late // g.tok) & (early < late), 1.0, 0.0).astype(BF16)
    rank = nn(named.astype(BF16), before)
    token = lax.broadcasted_iota(jnp.int32, (g.xy, g.col), 1)
    key = jnp.where(named > 0.0, rank + (CAP * (token // g.tok)).astype(F32), -1.0)
    slot = lax.broadcasted_iota(jnp.int32, (g.slots, g.col), 0).astype(F32)
    for d in range(g.xy):
        hit = key[d:d + 1, :] == slot
        pick[d * g.slots:(d + 1) * g.slots, :] = jnp.where(hit, 1.0, 0.0).astype(BF16)
        scaled[d * g.slots:(d + 1) * g.slots, :] = jnp.where(hit, weight[d:d + 1, :], 0.0).astype(BF16)

    mine = y * (g.nx // 2) + x // 2

    def to_plane(q, off, do):
        yy = lax.rem(y + off // g.nx, g.ny)
        xx = lax.rem(x + lax.rem(off, g.nx), g.nx)
        there = yy * g.nx + xx
        away = pltpu.make_async_remote_copy(
            sbuf.at[q, there], rbuf.at[c, q, mine], xy_send.at[q, off], xy_recv.at[c, q],
            device_id=(chip(yy, z, xx), parity), device_id_type=MESH,
        )
        stays = (off == 0) & (parity == c)

        @pl.when(jnp.logical_not(stays))
        def _():
            if do == "start":
                away.start()
            else:
                away.wait_send()

        if do == "start":
            @pl.when(stays)
            def _():
                pltpu.make_async_copy(sbuf.at[q, there], rbuf.at[c, q, mine], xy_recv.at[c, q]).start()

    def gather_and_send(q):
        rows = xall[q].reshape(g.col, g.dc)
        groups = 4
        per = g.xy // groups
        for i in range(groups):
            got = nn(pick[i * per * g.slots:(i + 1) * per * g.slots, :], rows).astype(BF16)
            sbuf[q, i * per:(i + 1) * per] = got.reshape(per, g.slots, g.dc)

        @pl.loop(0, g.xy)
        def _(off):
            to_plane(q, off, "start")

    for first in range(0, g.nq, 2):
        for step in range(1, g.nz // 2 + 1):
            for q in (first, first + 1):
                for way in range(2):
                    if step <= hops(q, way):
                        z_copy(q, way, step).wait_recv()
                        if step < hops(q, way):
                            z_copy(q, way, step + 1).start()
            if step == g.nz // 2 - 1 and first + 2 < g.nq:
                for q in (first + 2, first + 3):
                    for way in range(2):
                        z_copy(q, way, 1).start()
        for q in (first, first + 1):
            gather_and_send(q)
        if first == 0:
            same = jnp.where(early == late, 1.0, 0.0).astype(BF16)
            pick_t[...] = nt(same, pick[...]).astype(BF16)
            scaled_t[...] = nt(same, scaled[...]).astype(BF16)

    for i in range(3):
        weight_swap(i).wait()

    for q in range(g.nq):
        for kind in range(2):
            pltpu.make_async_copy(rbuf.at[kind, q], rbuf.at[kind, q], xy_recv.at[kind, q]).wait()
        rows = rbuf[0, q].reshape(g.rows, g.dc)
        grads = rbuf[1, q].reshape(g.rows, g.dc)
        feats = slice(q * g.dc, (q + 1) * g.dc)
        if q == 0:
            gacc[...] = nn(rows, wg[feats, :])
            uacc[...] = nn(rows, wu[feats, :])
            hacc[...] = nt(grads, wd[:, feats])
        else:
            gacc[...] += nn(rows, wg[feats, :])
            uacc[...] += nn(rows, wu[feats, :])
            hacc[...] += nt(grads, wd[:, feats])

    for i in range(g.src):
        span = slice(i * g.slots, (i + 1) * g.slots)
        gate_pre, up_pre, grad_hidden = gacc[span, :], uacc[span, :], hacc[span, :]
        sigma = jax.nn.sigmoid(gate_pre)
        down = grad_hidden * (gate_pre * sigma)
        score = jnp.sum(down * up_pre, axis=1, keepdims=True)
        wide = jnp.broadcast_to(score, (g.slots, LANES)).astype(BF16)
        for h in range(2):
            ret0[h, i, :, g.rc:] = wide
        gu[span, :] = down.astype(BF16)
        gg[span, :] = (grad_hidden * up_pre * sigma * (1.0 + gate_pre * (1.0 - sigma))).astype(BF16)

    here_d = y * g.nx + x

    def to_source(j, h, i, do):
        buf, dst = ((ret0, back0), (ret1, back1))[j]
        yy = i // (g.nx // 2)
        xx = 2 * lax.rem(i, g.nx // 2) + lax.rem(c + yy, 2)
        away = pltpu.make_async_remote_copy(
            buf.at[h, i], dst.at[here_d], ret_send.at[j, h, i], ret_recv.at[j],
            device_id=(chip(yy, z, xx), h), device_id_type=MESH,
        )
        stays = (xx == x) & (yy == y) & (c == h)

        @pl.when(jnp.logical_not(stays))
        def _():
            if do == "start":
                away.start()
            else:
                away.wait_send()

        if do == "start":
            @pl.when(stays)
            def _():
                pltpu.make_async_copy(buf.at[h, i], dst.at[here_d], ret_recv.at[j]).start()

    for j in range(2):
        buf = (ret0, ret1)[j]
        for h in range(2):
            feats = slice(h * g.dh + j * g.rc, h * g.dh + (j + 1) * g.rc)
            got = nt(gg[...], wg[feats, :]) + nt(gu[...], wu[feats, :])
            buf[h, :, :, :g.rc] = got.astype(BF16).reshape(g.src, g.slots, g.rc)
        for h in range(2):
            @pl.loop(0, g.src)
            def _(i):
                to_source(j, h, i, "start")

    def combine(j):
        dst = (back0, back1)[j]
        pltpu.make_async_copy(dst, dst, ret_recv.at[j]).wait()
        if j == 0:
            part0[:, :g.rc] = nn(scaled_t[...], back0[:, :, :g.rc].reshape(g.all_slots, g.rc))
            d = lax.broadcasted_iota(jnp.int32, (g.xy, g.slots, LANES), 0)
            at = lax.broadcasted_iota(jnp.int32, (g.xy, g.slots, LANES), 2)
            spot = ((d // g.nx) * g.nz + z) * g.nx + lax.rem(d, g.nx)
            score = jnp.where(at == spot, back0[:, :, g.rc:].astype(F32), 0.0).astype(BF16)
            part0[:, g.rc:] = nn(pick_t[...], score.reshape(g.all_slots, LANES))
        else:
            part1[...] = nn(scaled_t[...], back1[...].reshape(g.all_slots, g.rc))

    def own_part(j, block):
        part = (part0, part1)[j]
        return part[pl.ds(pl.multiple_of(block * g.tok, g.tok), g.tok), :]

    def rs_copy(j, way, step):
        sign = 1 - 2 * way
        src, dst = ((rsend0, rrecv0), (rsend1, rrecv1))[j]
        return pltpu.make_async_remote_copy(
            src.at[way, step - 1], dst.at[way, step - 1], rs_send.at[j, way, step - 1], rs_recv.at[j, way, step - 1],
            device_id=(chip(y, zmod(z + sign), x), c), device_id_type=MESH,
        )

    def rs_step(j, step):
        src, dst = ((rsend0, rrecv0), (rsend1, rrecv1))[j]
        for way in range(2):
            n = hops(j, way)
            if step > n:
                continue
            sign = 1 - 2 * way
            term = own_part(j, zmod(z + sign * (n + 1 - step)))
            if step > 1:
                rs_copy(j, way, step - 1).wait_recv()
                term = term + dst[way, step - 2].astype(F32)
            src[way, step - 1] = term.astype(BF16)
            rs_copy(j, way, step).start()

    def rs_last(j):
        dst = (rrecv0, rrecv1)[j]
        total = own_part(j, z)
        for way in range(2):
            n = hops(j, way)
            rs_copy(j, way, n).wait_recv()
            total = total + dst[way, n - 1].astype(F32)
        return total

    most = g.nz // 2
    combine(0)
    for step in range(1, most):
        rs_step(0, step)
    combine(1)
    rs_step(0, most)
    for step in range(1, most + 1):
        rs_step(1, step)
    first = rs_last(0)
    out_ref[c, :, :g.rc] = first[:, :g.rc].astype(BF16)
    scores = first[:, g.rc:]
    expert_at = lax.broadcasted_iota(jnp.int32, (g.tok, LANES), 1)
    gates = jnp.zeros((g.tok, LANES), F32)
    for k in range(g.top):
        one = jnp.sum(jnp.where(expert_at == ids_ref[:, k:k + 1], scores, 0.0), axis=1, keepdims=True)
        gates = jnp.where(expert_at == k, one, gates)
    gate_ref[...] = gates.astype(BF16)
    out_ref[c, :, g.rc:] = rs_last(1).astype(BF16)

    swap = pltpu.make_async_remote_copy(
        out_ref.at[c], out_ref.at[c], out_send, out_recv, device_id=(e, other), device_id_type=MESH
    )
    swap.start()

    for dz in range(1, g.nz):
        raw_copy(dz).wait_send()
    for q in range(g.nq):
        for way in range(2):
            for step in range(1, hops(q, way) + 1):
                z_copy(q, way, step).wait_send()

        @pl.loop(0, g.xy)
        def _(off):
            to_plane(q, off, "wait")
    for j in range(2):
        for h in range(2):
            @pl.loop(0, g.src)
            def _(i):
                to_source(j, h, i, "wait")
        for way in range(2):
            for step in range(1, hops(j, way) + 1):
                rs_copy(j, way, step).wait_send()
    swap.wait()


def scratch(g):
    dma = pltpu.SemaphoreType.DMA
    half = g.nz // 2
    vm = pltpu.VMEM
    return [
        vm((g.nq, g.nz, g.tok, g.dc), BF16),
        vm((g.nz, 16, LANES), F32),
        vm((g.all_slots, g.col), BF16),
        vm((g.all_slots, g.col), BF16),
        vm((g.col, g.all_slots), BF16),
        vm((g.col, g.all_slots), BF16),
        vm((g.nq, g.xy, g.slots, g.dc), BF16),
        vm((2, g.nq, g.src, g.slots, g.dc), BF16),
        vm((g.dim, g.ff), BF16),
        vm((g.dim, g.ff), BF16),
        vm((g.ff, g.dim), BF16),
        vm((g.rows, g.ff), F32),
        vm((g.rows, g.ff), F32),
        vm((g.rows, g.ff), F32),
        vm((g.rows, g.ff), BF16),
        vm((g.rows, g.ff), BF16),
        vm((2, g.src, g.slots, g.rc + LANES), BF16),
        vm((2, g.src, g.slots, g.rc), BF16),
        vm((g.xy, g.slots, g.rc + LANES), BF16),
        vm((g.xy, g.slots, g.rc), BF16),
        vm((g.col, g.rc + LANES), F32),
        vm((g.col, g.rc), F32),
        vm((2, half, g.tok, g.rc + LANES), BF16),
        vm((2, half, g.tok, g.rc), BF16),
        vm((2, half, g.tok, g.rc + LANES), BF16),
        vm((2, half, g.tok, g.rc), BF16),
        dma((g.nq,)),
        dma((3,)),
        dma((3,)),
        dma((3,)),
        dma((g.nz - 1,)),
        dma((g.nz - 1,)),
        dma((g.nq, 2, half)),
        dma((g.nq, 2, half)),
        dma((g.nq, g.xy)),
        dma((2, g.nq)),
        dma((2, 2, g.src)),
        dma((2,)),
        dma((2, 2, half)),
        dma((2, 2, half)),
        dma(()),
        dma(()),
    ]


def per_device(ny, nz, nx, chunks, tokens, cotangent, expert_ids, gate_weights, w_gate, w_up, w_down):
    tok, dim = tokens.shape
    top = expert_ids.shape[1]
    g = Sizes(tok, dim, w_gate.shape[2], top, ny, nz, nx, chunks)
    z = lax.rem(lax.axis_index("expert") // nx, nz)
    table = jnp.concatenate(
        [
            jnp.pad(expert_ids.astype(F32), ((0, 0), (0, 8 - top)), constant_values=-1.0),
            jnp.pad(gate_weights, ((0, 0), (0, 8 - top))),
        ],
        axis=1,
    ).T
    raw = jnp.where(
        lax.broadcasted_iota(jnp.int32, (16, 2 * tok), 1) // tok == z % 2, jnp.tile(table, (1, 2)), -1.0
    )
    vmem = pl.BlockSpec(memory_space=pltpu.VMEM)
    hbm = pl.BlockSpec(memory_space=pl.ANY)
    halves, gates = pl.pallas_call(
        functools.partial(kernel, g),
        out_shape=(
            jax.ShapeDtypeStruct((2, tok, g.dh), BF16),
            jax.ShapeDtypeStruct((tok, LANES), BF16),
        ),
        in_specs=[vmem, vmem, hbm, hbm, hbm, hbm, hbm],
        out_specs=(vmem, vmem),
        scratch_shapes=scratch(g),
        compiler_params=pltpu.CompilerParams(
            collective_id=0, has_side_effects=True, vmem_limit_bytes=60 * 1024 * 1024
        ),
    )(raw, expert_ids, tokens, cotangent, w_gate, w_up, w_down)
    return jnp.concatenate([halves[0], halves[1]], axis=1), gates[:, :top]


def solution(mesh, ny=NY, nz=NZ, nx=NX, chunks=4):
    placed = (
        P("expert", None),
        P("expert", None),
        P("expert", None),
        P("expert", None),
        P("expert", None, "half"),
        P("expert", None, "half"),
        P("expert", "half", None),
    )
    return jax.shard_map(
        functools.partial(per_device, ny, nz, nx, chunks),
        mesh=mesh,
        in_specs=placed,
        out_specs=(P("expert", None), P("expert", None)),
        check_vma=False,
    )
```

```python
import functools

import jax
import jax.numpy as jnp
from jax import lax
from jax.experimental import pallas as pl
from jax.experimental.pallas import tpu as pltpu
from jax.sharding import PartitionSpec as P

MESH = pl.DeviceIdType.MESH
F32 = jnp.float32
BF16 = jnp.bfloat16
NY, NZ, NX = 4, 8, 4
CAP = 6
LANES = 128


def nt(a, b):
    return lax.dot_general(a, b, (((1,), (1,)), ((), ())), preferred_element_type=F32)


def nn(a, b):
    return jnp.dot(a, b, preferred_element_type=F32)


class Sizes:
    def __init__(self, tok, dim, half_ff, top, ny, nz, nx, ahead, widths):
        self.tok, self.dim, self.hf, self.ff, self.top = tok, dim, half_ff, 2 * half_ff, top
        self.ny, self.nz, self.nx = ny, nz, nx
        self.ahead = ahead
        self.starts = [sum(ahead[:q]) for q in range(len(ahead))]
        self.nq = len(ahead)
        self.xy = ny * nx
        self.src = self.xy // 2
        self.slots = CAP * nz
        self.rows = self.src * self.slots
        self.all_slots = self.xy * self.slots
        self.col = nz * tok
        self.dh = dim // 2
        self.widths = widths
        self.cuts = [sum(widths[1:j]) for j in range(len(widths))]
        self.nj = len(widths)
        self.direct = self.nj - 1


def hops_of(number, way, half):
    return half if (number + way) % 2 == 0 else half - 1


def ring_plan(widths, half):
    lag, per_lane, fill = 2.1, 0.00275, 0.8
    link, now, waiting, plan = [0.0, 0.0], 0.0, [], []
    left = [2 * half - 1] * len(widths)
    fresh, tables = 0, False

    def send(q, way, step):
        link[way] = max(link[way], now) + per_lane * widths[q]
        waiting.append((link[way] + lag, q, way, step))

    while fresh < len(widths) or waiting:
        soonest = min(waiting)[0] if waiting else now
        if fresh < len(widths) and max(max(link), now) <= soonest:
            plan.append(("first", fresh))
            for way in range(2):
                send(fresh, way, 1)
            fresh += 1
            continue
        at, q, way, step = min(waiting)
        waiting.remove((at, q, way, step))
        now = max(now, at)
        if now > 4.4 and not tables:
            tables = True
            plan.append(("tables",))
        plan.append(("wait", q, way, step))
        if step < hops_of(q, way, half):
            send(q, way, step + 1)
        left[q] -= 1
        if not left[q]:
            plan.append(("gather", q))
            now += fill
    return plan


def sum_plan(widths, half, direct):
    now, plane, link = 0.0, 0.0, 0.0
    ready, made, plan = [], 0, []
    while made < len(widths) or ready:
        due = made < len(widths) and plane - now < 2.5
        soonest = min(ready) if ready else None
        if made < len(widths) and (due or soonest is None or soonest[0] > now):
            w = widths[made]
            plan.append(("make", made))
            now += 0.5 if made == 0 else 0.0078 * w
            plane = max(plane, now) + 0.0168 * w
            ready.append((plane + 1.5, made, 0))
            made += 1
            continue
        at, j, step = soonest
        ready.remove(soonest)
        now = max(now, at)
        w = widths[j]
        if step == 0:
            plan.append(("combine", j))
            now += 0.3 + 0.001 * w
        last = 1 if j == direct else half
        if step == last:
            plan.append(("last", j))
            now += 0.3
            continue
        if step:
            plan.append(("add", j, step + 1))
            now += 0.3
        link = max(link, now) + (0.022 if j == direct else 0.00275) * w
        ready.append((link + (4.0 if j == direct else 2.1), j, step + 1))
    return plan


def kernel(
    g, ids_hbm, gates_hbm, tok_hbm, cot_hbm, wg_hbm, wu_hbm, wd_hbm, out_ref, gate_ref,
    ids_ref, gates_ref, xall, rawall, pick, scaled, pick_t, scaled_t, sbuf, rbuf, wg, wu, wd, gacc, uacc, hacc, gg, gu,
    table_sem, own_sem, w_own_sem, w_send, w_recv, raw_send, raw_recv, z_send, z_recv, xy_send, xy_recv,
    ret_send, ret_recv, rs_send, rs_recv, out_send, out_recv, *lists,
):
    ret, back, part, rsend, rrecv = (lists[k * g.nj:(k + 1) * g.nj] for k in range(5))
    e = lax.axis_index("expert")
    c = lax.axis_index("half")
    x = lax.rem(e, g.nx)
    z = lax.rem(e // g.nx, g.nz)
    y = e // (g.nx * g.nz)
    other = 1 - c
    parity = lax.rem(x + y, 2)

    def chip(yy, zz, xx):
        return (yy * g.nz + zz) * g.nx + xx

    def zmod(v):
        return lax.rem(v + 2 * g.nz, g.nz)

    tables_in = (
        pltpu.make_async_copy(ids_hbm, ids_ref, table_sem.at[0]),
        pltpu.make_async_copy(gates_hbm, gates_ref, table_sem.at[1]),
    )
    for copy in tables_in:
        copy.start()

    @pl.when(c == 0)
    def _():
        pltpu.make_async_copy(tok_hbm, xall.at[z], own_sem).start()

    @pl.when(c == 1)
    def _():
        pltpu.make_async_copy(cot_hbm, xall.at[z], own_sem).start()

    cut = pl.ds(pl.multiple_of(c * g.hf, LANES), g.hf)
    places = (wg.at[:, cut], wu.at[:, cut], wd.at[cut, :])
    weights = (wg_hbm.at[0], wu_hbm.at[0], wd_hbm.at[0])

    def weight_own(i):
        return pltpu.make_async_copy(weights[i], places[i], w_own_sem.at[i])

    def weight_swap(i):
        return pltpu.make_async_remote_copy(
            places[i], places[i], w_send.at[i], w_recv.at[i], device_id=(e, other), device_id_type=MESH
        )

    barrier = pltpu.get_barrier_semaphore()
    for dz in range(1, g.nz):
        pl.semaphore_signal(barrier, inc=1, device_id=(chip(y, zmod(z + dz), x), c), device_id_type=MESH)
    for dy in range(g.ny):
        for dx in range(g.nx):
            peer = chip(lax.rem(y + dy, g.ny), z, lax.rem(x + dx, g.nx))
            if dy or dx:
                pl.semaphore_signal(barrier, inc=1, device_id=(peer, c), device_id_type=MESH)
            pl.semaphore_signal(barrier, inc=1, device_id=(peer, other), device_id_type=MESH)
    for i in range(3):
        weight_own(i).start()
    for copy in tables_in:
        copy.wait()
    table = jnp.concatenate([ids_ref[...].astype(F32), gates_ref[...]], axis=0)
    rawall[z] = jnp.concatenate([table, table], axis=1)
    pl.semaphore_wait(barrier, 2 * g.xy - 1 + g.nz - 1)

    def raw_copy(dz):
        return pltpu.make_async_remote_copy(
            rawall.at[z], rawall.at[z], raw_send, raw_recv,
            device_id=(chip(y, zmod(z + dz), x), c), device_id_type=MESH,
        )

    for dz in range(1, g.nz):
        raw_copy(dz).start()

    def hops(number, way):
        return hops_of(number, way, g.nz // 2)

    def lanes(q):
        return pl.ds(g.starts[q], g.ahead[q])

    def z_copy(q, way, step):
        sign = 1 - 2 * way
        rows = xall.at[zmod(z - sign * (step - 1)), :, lanes(q)]
        return pltpu.make_async_remote_copy(
            rows, rows, z_send, z_recv.at[q, way, step - 1],
            device_id=(chip(y, zmod(z + sign), x), c), device_id_type=MESH,
        )

    pltpu.make_async_copy(tok_hbm, xall.at[z], own_sem).wait()

    def tables():
        pltpu.make_async_copy(rawall.at[pl.ds(0, g.nz - 1)], rawall.at[pl.ds(0, g.nz - 1)], raw_recv).wait()
        lane = lax.broadcasted_iota(jnp.int32, (2 * g.top, LANES), 1)
        pairs = [
            jnp.where(lane < g.tok, rawall[2 * p], rawall[2 * p + 1]) for p in range(g.nz // 2)
        ]
        raw = jnp.concatenate(pairs, axis=1)
        place = lax.broadcasted_iota(jnp.int32, (g.xy, g.col), 0)
        named_by = (((place // g.nx) * g.nz + z) * g.nx + lax.rem(place, g.nx)).astype(F32)
        named = jnp.zeros((g.xy, g.col), F32)
        weight = jnp.zeros((g.xy, g.col), F32)
        for k in range(g.top):
            hit = raw[k:k + 1, :] == named_by
            named = named + jnp.where(hit, 1.0, 0.0)
            weight = weight + jnp.where(hit, raw[g.top + k:g.top + k + 1, :], 0.0)
        early = lax.broadcasted_iota(jnp.int32, (g.col, g.col), 0)
        late = lax.broadcasted_iota(jnp.int32, (g.col, g.col), 1)
        before = jnp.where((early // g.tok == late // g.tok) & (early < late), 1.0, 0.0).astype(BF16)
        rank = nn(named.astype(BF16), before)
        token = lax.broadcasted_iota(jnp.int32, (g.xy, g.col), 1)
        key = jnp.where(named > 0.0, rank + (CAP * (token // g.tok)).astype(F32), -1.0)
        slot = lax.broadcasted_iota(jnp.int32, (g.slots, g.col), 0).astype(F32)
        for d in range(g.xy):
            hit = key[d:d + 1, :] == slot
            pick[d * g.slots:(d + 1) * g.slots, :] = jnp.where(hit, 1.0, 0.0).astype(BF16)
            scaled[d * g.slots:(d + 1) * g.slots, :] = jnp.where(hit, weight[d:d + 1, :], 0.0).astype(BF16)

    mine = y * (g.nx // 2) + x // 2

    def to_plane(q, off):
        yy = lax.rem(y + off // g.nx, g.ny)
        xx = lax.rem(x + lax.rem(off, g.nx), g.nx)
        src = sbuf.at[yy * g.nx + xx, :, lanes(q)]
        dst = rbuf.at[c, mine, :, lanes(q)]
        stays = (off == 0) & (parity == c)

        @pl.when(jnp.logical_not(stays))
        def _():
            pltpu.make_async_remote_copy(
                src, dst, xy_send, xy_recv.at[c, q], device_id=(chip(yy, z, xx), parity), device_id_type=MESH
            ).start()

        @pl.when(stays)
        def _():
            pltpu.make_async_copy(src, dst, xy_recv.at[c, q]).start()

    def gather_and_send(q):
        rows = xall[:, :, g.starts[q]:g.starts[q] + g.ahead[q]].reshape(g.col, g.ahead[q])
        groups = 4
        per = g.xy // groups
        for i in range(groups):
            got = nn(pick[i * per * g.slots:(i + 1) * per * g.slots, :], rows).astype(BF16)
            sbuf[i * per:(i + 1) * per, :, g.starts[q]:g.starts[q] + g.ahead[q]] = got.reshape(per, g.slots, g.ahead[q])

        @pl.loop(0, g.xy)
        def _(off):
            to_plane(q, off)

    swapped = False
    for step in ring_plan(g.ahead, g.nz // 2):
        if step[0] == "first":
            for way in range(2):
                z_copy(step[1], way, 1).start()
        elif step[0] == "tables":
            tables()
        elif step[0] == "wait":
            _, q, way, at = step
            z_copy(q, way, at).wait_recv()
            if at < hops(q, way):
                z_copy(q, way, at + 1).start()
        else:
            gather_and_send(step[1])
            if not swapped:
                swapped = True
                for i in range(3):
                    weight_own(i).wait()
                    weight_swap(i).start()

    early = lax.broadcasted_iota(jnp.int32, (g.col, g.col), 0)
    late = lax.broadcasted_iota(jnp.int32, (g.col, g.col), 1)
    same = jnp.where(early == late, 1.0, 0.0).astype(BF16)
    pick_t[...] = nt(same, pick[...]).astype(BF16)
    scaled_t[...] = nt(same, scaled[...]).astype(BF16)

    for i in range(3):
        weight_swap(i).wait()

    for q in range(g.nq):
        feats = slice(g.starts[q], g.starts[q] + g.ahead[q])
        for kind in range(2):
            came = rbuf.at[kind, :, :, lanes(q)]
            pltpu.make_async_copy(came, came, xy_recv.at[kind, q]).wait()
        rows = rbuf[0, :, :, feats].reshape(g.rows, g.ahead[q])
        grads = rbuf[1, :, :, feats].reshape(g.rows, g.ahead[q])
        if q == 0:
            gacc[...] = nn(rows, wg[feats, :])
            uacc[...] = nn(rows, wu[feats, :])
            hacc[...] = nt(grads, wd[:, feats])
        else:
            gacc[...] += nn(rows, wg[feats, :])
            uacc[...] += nn(rows, wu[feats, :])
            hacc[...] += nt(grads, wd[:, feats])

    for i in range(g.src):
        span = slice(i * g.slots, (i + 1) * g.slots)
        gate_pre, up_pre, grad_hidden = gacc[span, :], uacc[span, :], hacc[span, :]
        sigma = jax.nn.sigmoid(gate_pre)
        down = grad_hidden * (gate_pre * sigma)
        score = jnp.sum(down * up_pre, axis=1, keepdims=True)
        wide = jnp.broadcast_to(score, (g.slots, LANES)).astype(BF16)
        ret[0][0, i] = wide
        gu[span, :] = down.astype(BF16)
        gg[span, :] = (grad_hidden * up_pre * sigma * (1.0 + gate_pre * (1.0 - sigma))).astype(BF16)

    here_d = y * g.nx + x

    def to_source(j, h, i):
        src = ret[j].at[h if j else 0, i]
        dst = back[j].at[here_d]
        yy = i // (g.nx // 2)
        xx = 2 * lax.rem(i, g.nx // 2) + lax.rem(c + yy, 2)
        stays = (xx == x) & (yy == y) & (c == h)

        @pl.when(jnp.logical_not(stays))
        def _():
            pltpu.make_async_remote_copy(
                src, dst, ret_send.at[j], ret_recv.at[j], device_id=(chip(yy, z, xx), h), device_id_type=MESH
            ).start()

        @pl.when(stays)
        def _():
            pltpu.make_async_copy(src, dst, ret_recv.at[j]).start()

    def make(j):
        for h in range(2):
            if j:
                feats = slice(h * g.dh + g.cuts[j], h * g.dh + g.cuts[j] + g.widths[j])
                got = nt(gg[...], wg[feats, :]) + nt(gu[...], wu[feats, :])
                ret[j][h] = got.astype(BF16).reshape(g.src, g.slots, g.widths[j])

            @pl.loop(0, g.src)
            def _(i):
                to_source(j, h, i)

    def combine(j):
        pltpu.make_async_copy(back[j], back[j], ret_recv.at[j]).wait()
        if j == 0:
            d = lax.broadcasted_iota(jnp.int32, (g.xy, g.slots, LANES), 0)
            at = lax.broadcasted_iota(jnp.int32, (g.xy, g.slots, LANES), 2)
            spot = ((d // g.nx) * g.nz + z) * g.nx + lax.rem(d, g.nx)
            score = jnp.where(at == spot, back[0][...].astype(F32), 0.0).astype(BF16)
            part[0][...] = nn(pick_t[...], score.reshape(g.all_slots, LANES))
        else:
            part[j][...] = nn(scaled_t[...], back[j][...].reshape(g.all_slots, g.widths[j]))

    def own_part(j, block):
        return part[j][pl.ds(pl.multiple_of(block * g.tok, g.tok), g.tok), :]

    def spot(j, way, step):
        return step - 1 + way * hops(j, 0)

    def rs_copy(j, way, step):
        sign = 1 - 2 * way
        n = spot(j, way, step)
        return pltpu.make_async_remote_copy(
            rsend[j].at[n], rrecv[j].at[n], rs_send.at[j], rs_recv.at[j, n],
            device_id=(chip(y, zmod(z + sign), x), c), device_id_type=MESH,
        )

    def rs_step(j, step):
        for way in range(2):
            n = hops(j, way)
            if step > n:
                continue
            sign = 1 - 2 * way
            term = own_part(j, zmod(z + sign * (n + 1 - step)))
            if step > 1:
                rs_copy(j, way, step - 1).wait_recv()
                term = term + rrecv[j][spot(j, way, step - 1)].astype(F32)
            rsend[j][spot(j, way, step)] = term.astype(BF16)
            rs_copy(j, way, step).start()

    def rs_direct(j):
        for dz in sorted(range(1, g.nz), key=lambda v: -min(v, g.nz - v)):
            there = zmod(z + dz)
            rsend[j][dz - 1] = own_part(j, there).astype(BF16)
            pltpu.make_async_remote_copy(
                rsend[j].at[dz - 1], rrecv[j].at[dz - 1], rs_send.at[j], rs_recv.at[j, 0],
                device_id=(chip(y, there, x), c), device_id_type=MESH,
            ).start()

    def swap(j):
        span = pl.ds(pl.multiple_of(c * g.dh + g.cuts[j], LANES), g.widths[j])
        return pltpu.make_async_remote_copy(
            out_ref.at[:, span], out_ref.at[:, span], out_send, out_recv,
            device_id=(e, other), device_id_type=MESH,
        )

    def rs_last(j):
        total = own_part(j, z)
        if j == g.direct:
            pltpu.make_async_copy(rrecv[j], rrecv[j], rs_recv.at[j, 0]).wait()
            for n in range(g.nz - 1):
                total = total + rrecv[j][n].astype(F32)
        else:
            for way in range(2):
                rs_copy(j, way, hops(j, way)).wait_recv()
                total = total + rrecv[j][spot(j, way, hops(j, way))].astype(F32)
        if j:
            out_ref[:, pl.ds(pl.multiple_of(c * g.dh + g.cuts[j], LANES), g.widths[j])] = total.astype(BF16)
            swap(j).start()
        else:
            square = (LANES, LANES)
            same = lax.broadcasted_iota(jnp.int32, square, 0) == lax.broadcasted_iota(jnp.int32, square, 1)
            scores = nt(jnp.where(same, 1.0, 0.0).astype(BF16), total.astype(BF16))
            expert_at = lax.broadcasted_iota(jnp.int32, (LANES, g.tok), 0)
            for k in range(g.top):
                one = jnp.where(expert_at == ids_ref[k:k + 1, :], scores, 0.0)
                gate_ref[k:k + 1, :] = jnp.sum(one, axis=0, keepdims=True)

    for step in sum_plan(g.widths, g.nz // 2, g.direct):
        if step[0] == "make":
            make(step[1])
        elif step[0] == "combine":
            combine(step[1])
            if step[1] == g.direct:
                rs_direct(step[1])
            else:
                rs_step(step[1], 1)
        elif step[0] == "add":
            rs_step(step[1], step[2])
        else:
            rs_last(step[1])

    def gone(ref, sem):
        pltpu.make_async_copy(ref, ref, sem).wait()

    some = pl.ds(0, g.nz - 1)
    gone(rawall.at[some], raw_send)
    gone(xall.at[some], z_send)
    for j in range(g.nj):
        gone(rsend[j], rs_send.at[j])

    @pl.when(parity == c)
    def _():
        fewer = pl.ds(0, g.xy - 1)
        gone(sbuf.at[fewer], xy_send)
        for j in range(g.nj):
            gone(back[j].at[fewer], ret_send.at[j])

    @pl.when(parity != c)
    def _():
        gone(sbuf, xy_send)
        for j in range(g.nj):
            gone(back[j], ret_send.at[j])

    half = out_ref.at[:, pl.ds(0, g.dh)]
    gone(half, out_send)
    gone(half, out_recv)


def scratch(g):
    dma = pltpu.SemaphoreType.DMA
    half = g.nz // 2
    vm = pltpu.VMEM
    return [
        vm((g.top, g.tok), jnp.int32),
        vm((g.top, g.tok), F32),
        vm((g.nz, g.tok, g.dim), BF16),
        vm((g.nz, 2 * g.top, LANES), F32),
        vm((g.all_slots, g.col), BF16),
        vm((g.all_slots, g.col), BF16),
        vm((g.col, g.all_slots), BF16),
        vm((g.col, g.all_slots), BF16),
        vm((g.xy, g.slots, g.dim), BF16),
        vm((2, g.src, g.slots, g.dim), BF16),
        vm((g.dim, g.ff), BF16),
        vm((g.dim, g.ff), BF16),
        vm((g.ff, g.dim), BF16),
        vm((g.rows, g.ff), F32),
        vm((g.rows, g.ff), F32),
        vm((g.rows, g.ff), F32),
        vm((g.rows, g.ff), BF16),
        vm((g.rows, g.ff), BF16),
        dma((2,)),
        dma(()),
        dma((3,)),
        dma((3,)),
        dma((3,)),
        dma(()),
        dma(()),
        dma(()),
        dma((g.nq, 2, half)),
        dma(()),
        dma((2, g.nq)),
        dma((g.nj,)),
        dma((g.nj,)),
        dma((g.nj,)),
        dma((g.nj, g.nz - 1)),
        dma(()),
        dma(()),
        *[vm((2 if j else 1, g.src, g.slots, w), BF16) for j, w in enumerate(g.widths)],
        *[vm((g.xy, g.slots, w), BF16) for w in g.widths],
        *[vm((g.col, w), F32) for w in g.widths],
        *[vm((g.nz - 1, g.tok, w), BF16) for w in g.widths],
        *[vm((g.nz - 1, g.tok, w), BF16) for w in g.widths],
    ]


def per_device(ny, nz, nx, ahead, widths, tokens, cotangent, expert_ids, gate_weights, w_gate, w_up, w_down):
    tok, dim = tokens.shape
    top = expert_ids.shape[1]
    g = Sizes(tok, dim, w_gate.shape[2], top, ny, nz, nx, ahead, widths)
    vmem = pl.BlockSpec(memory_space=pltpu.VMEM)
    hbm = pl.BlockSpec(memory_space=pl.ANY)
    input_grad, gate_grad = pl.pallas_call(
        functools.partial(kernel, g),
        out_shape=(
            jax.ShapeDtypeStruct((tok, dim), BF16),
            jax.ShapeDtypeStruct((top, tok), F32),
        ),
        in_specs=[hbm] * 7,
        out_specs=(vmem, vmem),
        scratch_shapes=scratch(g),
        compiler_params=pltpu.CompilerParams(
            collective_id=0, has_side_effects=True, vmem_limit_bytes=60 * 1024 * 1024
        ),
    )(expert_ids.T, gate_weights.T, tokens, cotangent, w_gate, w_up, w_down)
    return input_grad, gate_grad.T.astype(BF16)


def solution(mesh, ny=NY, nz=NZ, nx=NX, ahead=(128, 128) + (256,) * 7, widths=(LANES, 128, 256, 256, 256, 128)):
    placed = (
        P("expert", None),
        P("expert", None),
        P("expert", None),
        P("expert", None),
        P("expert", None, "half"),
        P("expert", None, "half"),
        P("expert", "half", None),
    )
    return jax.shard_map(
        functools.partial(per_device, ny, nz, nx, ahead, widths),
        mesh=mesh,
        in_specs=placed,
        out_specs=(P("expert", None), P("expert", None)),
        check_vma=False,
    )
```

```python
import functools

import jax
import jax.numpy as jnp
from jax import lax
from jax.experimental import pallas as pl
from jax.experimental.pallas import tpu as pltpu
from jax.sharding import PartitionSpec as P

MESH = pl.DeviceIdType.MESH
F32 = jnp.float32
BF16 = jnp.bfloat16
NY, NZ, NX = 4, 8, 4
CAP = 6
LANES = 128


def nt(a, b):
    return lax.dot_general(a, b, (((1,), (1,)), ((), ())), preferred_element_type=F32)


def nn(a, b):
    return jnp.dot(a, b, preferred_element_type=F32)


class Sizes:
    def at(self, away):
        return self.order.index(away % self.nz)

    def __init__(self, tok, dim, half_ff, top, ny, nz, nx, ahead, near, widths, direct):
        self.tok, self.dim, self.hf, self.ff, self.top = tok, dim, half_ff, 2 * half_ff, top
        self.ny, self.nz, self.nx = ny, nz, nx
        self.ahead = ahead
        self.starts = [sum(ahead[:q]) for q in range(len(ahead))]
        self.nq = len(ahead)
        self.near = near
        self.order = [0] + [v for k in range(1, nz // 2) for v in (k, nz - k)] + [nz // 2]
        self.early = 16
        self.reach = 3
        self.xy = ny * nx
        self.src = self.xy // 2
        self.slots = CAP * nz
        self.rows = self.src * self.slots
        self.all_slots = self.xy * self.slots
        self.col = nz * tok
        self.dh = dim // 2
        self.widths = widths
        self.cuts = [sum(widths[1:j]) for j in range(len(widths))]
        self.nj = len(widths)
        self.direct = direct


def hops_of(number, way, half):
    return half if (number + way) % 2 == 0 else half - 1


def ring_plan(widths, near, half):
    lag, per_lane, hop = 2.3, 0.0036, 2.9
    size = [0.0]
    for w in widths:
        size.append(size[-1] + w / sum(widths))
    sends, came = [], {}
    for way in range(2):
        ready = {(q, 1): 0.0 for q in range(len(widths))}
        link = 0.0
        while ready:
            def due(item):
                q, step = item
                last = 15.5 + 23.0 * size[q] - hop * (hops_of(q, way, half) - step)
                return min(last, 4.0 + 11.4 * size[q]) if step == 1 else last

            now = max(link, min(ready.values()))
            q, step = min((item for item in ready if ready[item] <= now), key=due)
            del ready[q, step]
            sends.append((now, 0, "send", q, way, step))
            link = now + per_lane * widths[q]
            came[q, way, step] = link + lag
            if step < hops_of(q, way, half):
                ready[q, step + 1] = link + lag
    events = [(4.4, 1, "tables")]
    first = [max(came[q, way, 1] for q in group for way in range(2)) for group in near]
    events += [(max(4.9, t), 2, "near", n) for n, t in enumerate(first)]
    latest = max(4.9, max(first))
    for q in range(len(widths)):
        t = max(v for k, v in came.items() if k[0] == q)
        events.append((max(t, latest + 0.01), 3, "far", q))
    return [event[2:] for event in sorted(sends + events)]


def sum_plan(widths, half, direct, early):
    count = len(widths)
    plan, events, now, plane, link = [], [], 0.0, 0.0, 0.0
    for j in [1, 0, *range(2, count)]:
        plan.append(("make", j))
        now += 1.8 if j else 0.4
        plane = max(plane, now) + (0.0168 * widths[j] * (1.0 - early) if j else 0.7)
        events.append((plane + 3.8, "combine", j, 0))
    close = [0.0] * count
    for j in range(1, count):
        plan.append(("near", j))
        now += 0.4
        plane = max(plane, now) + 0.0168 * widths[j] * early
        close[j] = plane + 3.8
    while events:
        at, kind, j, step = min(events)
        events.remove((at, kind, j, step))
        now = max(now, at)
        plan.append((kind, j, step))
        now += {"combine": 0.5, "add": 0.25, "close": 0.6, "last": 0.3}[kind]
        if kind == "last":
            continue
        if j in direct:
            units = 7.0 if kind == "combine" else 1.0
        else:
            units = 1.0
        link = max(link, now) + 0.0036 * units * widths[j]
        there = link + (4.1 if j in direct and kind == "combine" else 2.3)
        hops = half if j == 0 else half - 1
        if kind == "close" or (j == 0 and step == hops - 1):
            events.append((there, "last", j, 0))
        elif j in direct or step == hops - 1:
            events.append((close[j] if j in direct else max(close[j], there), "close", j, 0))
        else:
            events.append((there, "add", j, step + 1))
    return plan


def kernel(
    g, ids_hbm, gates_hbm, tok_hbm, cot_hbm, wg_hbm, wu_hbm, wd_hbm, out_ref, gate_ref,
    ids_ref, gates_ref, xall, rawall, pick_near, pick_far, pick, scaled, pick_t, near_t, far_t, sbuf, rbuf, wg, wu, wd, gacc, uacc, hacc, gg, gu,
    table_sem, own_sem, w_own_sem, w_send, w_recv, raw_send, raw_recv, z_send, z_recv, xy_send, near_recv, xy_recv,
    ret_send, ret_recv, back_recv, rs_send, rs_recv, out_send, out_recv, *lists,
):
    ret, back, part, rsend, rrecv = (lists[k * g.nj:(k + 1) * g.nj] for k in range(5))
    e = lax.axis_index("expert")
    c = lax.axis_index("half")
    x = lax.rem(e, g.nx)
    z = lax.rem(e // g.nx, g.nz)
    y = e // (g.nx * g.nz)
    other = 1 - c
    parity = lax.rem(x + y, 2)

    def chip(yy, zz, xx):
        return (yy * g.nz + zz) * g.nx + xx

    def zmod(v):
        return lax.rem(v + 2 * g.nz, g.nz)

    tables_in = (
        pltpu.make_async_copy(ids_hbm, ids_ref, table_sem.at[0]),
        pltpu.make_async_copy(gates_hbm, gates_ref, table_sem.at[1]),
    )
    for copy in tables_in:
        copy.start()

    @pl.when(c == 0)
    def _():
        pltpu.make_async_copy(tok_hbm, xall.at[0], own_sem).start()

    @pl.when(c == 1)
    def _():
        pltpu.make_async_copy(cot_hbm, xall.at[0], own_sem).start()

    cut = pl.ds(pl.multiple_of(c * g.hf, LANES), g.hf)
    places = (wg.at[:, cut], wu.at[:, cut], wd.at[cut, :])
    weights = (wg_hbm.at[0], wu_hbm.at[0], wd_hbm.at[0])

    def weight_own(i):
        return pltpu.make_async_copy(weights[i], places[i], w_own_sem.at[i])

    def weight_swap(i):
        return pltpu.make_async_remote_copy(
            places[i], places[i], w_send.at[i], w_recv.at[i], device_id=(e, other), device_id_type=MESH
        )

    barrier = pltpu.get_barrier_semaphore()
    for dz in range(1, g.nz):
        pl.semaphore_signal(barrier, inc=1, device_id=(chip(y, zmod(z + dz), x), c), device_id_type=MESH)
    for dy in range(g.ny):
        for dx in range(g.nx):
            peer = chip(lax.rem(y + dy, g.ny), z, lax.rem(x + dx, g.nx))
            if dy or dx:
                pl.semaphore_signal(barrier, inc=1, device_id=(peer, c), device_id_type=MESH)
            pl.semaphore_signal(barrier, inc=1, device_id=(peer, other), device_id_type=MESH)
    for i in range(3):
        weight_own(i).start()
    for copy in tables_in:
        copy.wait()
    table = jnp.concatenate([ids_ref[...].astype(F32), gates_ref[...]], axis=0)
    rawall[0] = jnp.concatenate([table, table], axis=1)
    pl.semaphore_wait(barrier, 2 * g.xy - 1 + g.nz - 1)

    def raw_copy(dz):
        return pltpu.make_async_remote_copy(
            rawall.at[0], rawall.at[g.at(-dz)], raw_send, raw_recv,
            device_id=(chip(y, zmod(z + dz), x), c), device_id_type=MESH,
        )

    for dz in range(1, g.nz):
        raw_copy(dz).start()

    def hops(number, way):
        return hops_of(number, way, g.nz // 2)

    def lanes(q):
        return pl.ds(g.starts[q], g.ahead[q])

    def z_copy(q, way, step):
        sign = 1 - 2 * way
        src = xall.at[g.at(-sign * (step - 1)), :, lanes(q)]
        dst = xall.at[g.at(-sign * step), :, lanes(q)]
        return pltpu.make_async_remote_copy(
            src, dst, z_send, z_recv.at[q, way, step - 1],
            device_id=(chip(y, zmod(z + sign), x), c), device_id_type=MESH,
        )

    pltpu.make_async_copy(tok_hbm, xall.at[0], own_sem).wait()

    def tables():
        pltpu.make_async_copy(rawall.at[pl.ds(1, g.nz - 1)], rawall.at[pl.ds(1, g.nz - 1)], raw_recv).wait()
        lane = lax.broadcasted_iota(jnp.int32, (2 * g.top, LANES), 1)
        pairs = [
            jnp.where(lane < g.tok, rawall[2 * p], rawall[2 * p + 1]) for p in range(g.nz // 2)
        ]
        raw = jnp.concatenate(pairs, axis=1)
        place = lax.broadcasted_iota(jnp.int32, (g.xy, g.col), 0)
        named_by = (((place // g.nx) * g.nz + z) * g.nx + lax.rem(place, g.nx)).astype(F32)
        named = jnp.zeros((g.xy, g.col), F32)
        weight = jnp.zeros((g.xy, g.col), F32)
        for k in range(g.top):
            hit = raw[k:k + 1, :] == named_by
            named = named + jnp.where(hit, 1.0, 0.0)
            weight = weight + jnp.where(hit, raw[g.top + k:g.top + k + 1, :], 0.0)
        early = lax.broadcasted_iota(jnp.int32, (g.col, g.col), 0)
        late = lax.broadcasted_iota(jnp.int32, (g.col, g.col), 1)
        before = jnp.where((early // g.tok == late // g.tok) & (early < late), 1.0, 0.0).astype(BF16)
        rank = nn(named.astype(BF16), before)
        token = lax.broadcasted_iota(jnp.int32, (g.xy, g.col), 1)
        key = jnp.where(named > 0.0, rank + (CAP * (token // g.tok)).astype(F32), -1.0)
        slot = lax.broadcasted_iota(jnp.int32, (g.slots, g.col), 0).astype(F32)
        for d in range(g.xy):
            hit = key[d:d + 1, :] == slot
            pick[d * g.slots:(d + 1) * g.slots, :] = jnp.where(hit, 1.0, 0.0).astype(BF16)
            scaled[d * g.slots:(d + 1) * g.slots, :] = jnp.where(hit, weight[d:d + 1, :], 0.0).astype(BF16)

        whole = pick[...].reshape(g.xy, g.slots, g.col)
        pick_near[...] = whole[:, :g.early, :g.reach * g.tok].reshape(g.xy * g.early, g.reach * g.tok)
        late_slots = g.slots - g.early
        pick_far[...] = whole[:, g.early:, (g.reach - 1) * g.tok:].reshape(g.xy * late_slots, g.col - (g.reach - 1) * g.tok)

    mine = y * (g.nx // 2) + x // 2

    def to_plane(rows, span, sem, off):
        yy = lax.rem(y + off // g.nx, g.ny)
        xx = lax.rem(x + lax.rem(off, g.nx), g.nx)
        src = sbuf.at[yy * g.nx + xx, rows, span]
        dst = rbuf.at[c, mine, rows, span]
        stays = (off == 0) & (parity == c)

        @pl.when(jnp.logical_not(stays))
        def _():
            pltpu.make_async_remote_copy(
                src, dst, xy_send, sem, device_id=(chip(yy, z, xx), parity), device_id_type=MESH
            ).start()

        @pl.when(stays)
        def _():
            pltpu.make_async_copy(src, dst, sem).start()

    early_rows, late_rows = pl.ds(0, g.early), pl.ds(g.early, g.slots - g.early)

    def near_span(n):
        return g.starts[g.near[n][0]], sum(g.ahead[q] for q in g.near[n])

    def gather_near(n):
        start, width = near_span(n)
        rows = xall[:g.reach, :, start:start + width].reshape(g.reach * g.tok, width)
        got = nn(pick_near[...], rows).astype(BF16)
        sbuf[:, :g.early, start:start + width] = got.reshape(g.xy, g.early, width)

        @pl.loop(0, g.xy)
        def _(off):
            to_plane(early_rows, pl.ds(start, width), near_recv.at[c, n], off)

    def gather_far(q):
        start, width = g.starts[q], g.ahead[q]
        rows = xall[g.reach - 1:, :, start:start + width].reshape(g.col - (g.reach - 1) * g.tok, width)
        groups = 4
        per = g.xy // groups
        late = g.slots - g.early
        for i in range(groups):
            got = nn(pick_far[i * per * late:(i + 1) * per * late, :], rows).astype(BF16)
            sbuf[i * per:(i + 1) * per, g.early:, start:start + width] = got.reshape(per, late, width)

        @pl.loop(0, g.xy)
        def _(off):
            to_plane(late_rows, pl.ds(start, width), xy_recv.at[c, q], off)

    arrived = set()

    def need(q, steps):
        for at in steps:
            for way in range(2):
                if at <= hops(q, way) and (q, way, at) not in arrived:
                    arrived.add((q, way, at))
                    z_copy(q, way, at).wait_recv()

    def need_one(q, way, at):
        if at and (q, way, at) not in arrived:
            arrived.add((q, way, at))
            z_copy(q, way, at).wait_recv()

    swapped = False
    for step in ring_plan(g.ahead, g.near, g.nz // 2):
        if step[0] == "send":
            _, q, way, at = step
            need_one(q, way, at - 1)
            z_copy(q, way, at).start()
        elif step[0] == "tables":
            tables()
        elif step[0] == "near":
            for q in g.near[step[1]]:
                need(q, (1,))
            gather_near(step[1])
            if not swapped:
                swapped = True
                for i in range(3):
                    weight_own(i).wait()
                    weight_swap(i).start()
        else:
            need(step[1], range(1, g.nz // 2 + 1))
            gather_far(step[1])

    early = lax.broadcasted_iota(jnp.int32, (g.col, g.col), 0)
    late = lax.broadcasted_iota(jnp.int32, (g.col, g.col), 1)
    same = jnp.where(early == late, 1.0, 0.0).astype(BF16)
    pick_t[...] = nt(same, pick[...]).astype(BF16)
    whole = scaled[...].reshape(g.xy, g.slots, g.col)
    near_cols, far_cols = g.reach * g.tok, g.col - (g.reach - 1) * g.tok
    near_t[...] = nt(same[:near_cols, :near_cols], whole[:, :g.early, :near_cols].reshape(g.xy * g.early, near_cols)).astype(BF16)
    far_slots = whole[:, g.early:, g.col - far_cols:].reshape(g.xy * (g.slots - g.early), far_cols)
    far_t[...] = nt(same[:far_cols, :far_cols], far_slots).astype(BF16)

    for i in range(3):
        weight_swap(i).wait()

    for q in range(g.nq):
        feats = slice(g.starts[q], g.starts[q] + g.ahead[q])
        for n, group in enumerate(g.near):
            if q == group[0]:
                start, width = near_span(n)
                for kind in range(2):
                    came = rbuf.at[kind, :, early_rows, pl.ds(start, width)]
                    pltpu.make_async_copy(came, came, near_recv.at[kind, n]).wait()
        for kind in range(2):
            came = rbuf.at[kind, :, late_rows, lanes(q)]
            pltpu.make_async_copy(came, came, xy_recv.at[kind, q]).wait()
        rows = rbuf[0, :, :, feats].reshape(g.rows, g.ahead[q])
        grads = rbuf[1, :, :, feats].reshape(g.rows, g.ahead[q])
        if q == 0:
            gacc[...] = nn(rows, wg[feats, :])
            uacc[...] = nn(rows, wu[feats, :])
            hacc[...] = nt(grads, wd[:, feats])
        else:
            gacc[...] += nn(rows, wg[feats, :])
            uacc[...] += nn(rows, wu[feats, :])
            hacc[...] += nt(grads, wd[:, feats])

    for i in range(g.src):
        span = slice(i * g.slots, (i + 1) * g.slots)
        gate_pre, up_pre, grad_hidden = gacc[span, :], uacc[span, :], hacc[span, :]
        sigma = jax.nn.sigmoid(gate_pre)
        down = grad_hidden * (gate_pre * sigma)
        score = jnp.sum(down * up_pre, axis=1, keepdims=True)
        wide = jnp.broadcast_to(score, (g.slots, LANES)).astype(BF16)
        first = jnp.where(lax.broadcasted_iota(jnp.int32, (16, LANES), 1) == 0, 1.0, 0.0).astype(BF16)
        ret[0][0, i, :, :g.slots] = nt(first, wide).astype(BF16)
        gu[span, :] = down.astype(BF16)
        gg[span, :] = (grad_hidden * up_pre * sigma * (1.0 + gate_pre * (1.0 - sigma))).astype(BF16)

    here_d = y * g.nx + x

    def to_source(j, h, i, rows, sem):
        dy = i // (g.nx // 2)
        dx = 2 * lax.rem(i, g.nx // 2) + lax.rem(dy + parity + c, 2)
        yy = lax.rem(y + dy, g.ny)
        xx = lax.rem(x + dx, g.nx)
        src = ret[j].at[h if j else 0, yy * (g.nx // 2) + xx // 2, rows]
        dst = back[j].at[here_d, rows]
        stays = (xx == x) & (yy == y) & (c == h)

        @pl.when(jnp.logical_not(stays))
        def _():
            pltpu.make_async_remote_copy(
                src, dst, ret_send.at[j], sem, device_id=(chip(yy, z, xx), h), device_id_type=MESH
            ).start()

        @pl.when(stays)
        def _():
            pltpu.make_async_copy(src, dst, sem).start()

    def send_back(j, rows, sem):
        @pl.loop(0, g.src)
        def _(i):
            for h in range(2):
                to_source(j, h, i, rows, sem)

    def make(j):
        w = g.widths[j]
        if j:
            cuts = [h * g.dh + g.cuts[j] for h in range(2)]
            both = [jnp.concatenate([ref[cut:cut + w, :] for cut in cuts], axis=0) for ref in (wg, wu)]
            got = (nt(gg[...], both[0]) + nt(gu[...], both[1])).astype(BF16)
            for h in range(2):
                ret[j][h] = got[:, h * w:(h + 1) * w].reshape(g.src, g.slots, w)

        send_back(j, late_rows if j else pl.ds(0, 16), ret_recv.at[j])

    def combine(j):
        came = back[j].at[:, late_rows if j else pl.ds(0, 16)]
        pltpu.make_async_copy(came, came, ret_recv.at[j]).wait()
        if j == 0:
            slot = lax.broadcasted_iota(jnp.int32, (g.slots, g.slots), 0)
            same = jnp.where(slot == lax.broadcasted_iota(jnp.int32, (g.slots, g.slots), 1), 1.0, 0.0).astype(BF16)
            at = lax.broadcasted_iota(jnp.int32, (g.slots, LANES), 1)
            placed = []
            for d in range(g.xy):
                column = nt(same, back[0][d, :, :g.slots])[:, :1]
                expert = ((d // g.nx) * g.nz + z) * g.nx + d % g.nx
                placed.append(jnp.where(at == expert, column, 0.0).astype(BF16))
            part[0][...] = nn(pick_t[...], jnp.concatenate(placed, axis=0))
        else:
            late = g.slots - g.early
            part[j][(g.reach - 1) * g.tok:, :] = nn(far_t[...], back[j][:, g.early:, :].reshape(g.xy * late, g.widths[j]))

    def combine_near(j):
        came = back[j].at[:, early_rows]
        pltpu.make_async_copy(came, came, back_recv.at[j]).wait()
        got = nn(near_t[...], back[j][:, :g.early, :].reshape(g.xy * g.early, g.widths[j]))
        edge = (g.reach - 1) * g.tok
        part[j][:edge, :] = got[:edge]
        part[j][edge:edge + g.tok, :] += got[edge:]

    def own_part(j, away):
        block = g.at(away)
        return part[j][block * g.tok:(block + 1) * g.tok, :]

    def spot(j, way, step):
        return step - 1 + way * hops(j, 0)

    def rs_copy(j, way, step):
        sign = 1 - 2 * way
        n = spot(j, way, step)
        return pltpu.make_async_remote_copy(
            rsend[j].at[n], rrecv[j].at[n], rs_send.at[j], rs_recv.at[j, n],
            device_id=(chip(y, zmod(z + sign), x), c), device_id_type=MESH,
        )

    def rs_step(j, step, last):
        for way in range(2):
            n = hops(j, way)
            at = n if last else step
            if at > n or (at == n and j and not last):
                continue
            sign = 1 - 2 * way
            term = own_part(j, sign * (n + 1 - at))
            if at > 1:
                rs_copy(j, way, at - 1).wait_recv()
                term = term + rrecv[j][spot(j, way, at - 1)].astype(F32)
            rsend[j][spot(j, way, at)] = term.astype(BF16)
            rs_copy(j, way, at).start()

    def rs_direct(j, away, sem):
        for dz in away:
            rsend[j][dz - 1] = own_part(j, dz).astype(BF16)
            pltpu.make_async_remote_copy(
                rsend[j].at[dz - 1], rrecv[j].at[dz - 1], rs_send.at[j], rs_recv.at[j, sem + (dz == g.nz - 1)],
                device_id=(chip(y, zmod(z + dz), x), c), device_id_type=MESH,
            ).start()

    far_away = sorted(range(2, g.nz - 1), key=lambda v: -min(v, g.nz - v))

    def swap(j):
        span = pl.ds(pl.multiple_of(c * g.dh + g.cuts[j], LANES), g.widths[j])
        return pltpu.make_async_remote_copy(
            out_ref.at[:, span], out_ref.at[:, span], out_send, out_recv,
            device_id=(e, other), device_id_type=MESH,
        )

    def rs_last(j):
        total = own_part(j, 0)
        if j in g.direct:
            for n, some in enumerate((pl.ds(1, g.nz - 3), pl.ds(0, 1), pl.ds(g.nz - 2, 1))):
                pltpu.make_async_copy(rrecv[j].at[some], rrecv[j].at[some], rs_recv.at[j, n]).wait()
            for n in range(g.nz - 1):
                total = total + rrecv[j][n].astype(F32)
        else:
            for way in range(2):
                rs_copy(j, way, hops(j, way)).wait_recv()
                total = total + rrecv[j][spot(j, way, hops(j, way))].astype(F32)
        if j:
            out_ref[:, pl.ds(pl.multiple_of(c * g.dh + g.cuts[j], LANES), g.widths[j])] = total.astype(BF16)
            swap(j).start()
        else:
            square = (LANES, LANES)
            same = lax.broadcasted_iota(jnp.int32, square, 0) == lax.broadcasted_iota(jnp.int32, square, 1)
            scores = nt(jnp.where(same, 1.0, 0.0).astype(BF16), total.astype(BF16))
            expert_at = lax.broadcasted_iota(jnp.int32, (LANES, g.tok), 0)
            for k in range(g.top):
                one = jnp.where(expert_at == ids_ref[k:k + 1, :], scores, 0.0)
                gate_ref[k:k + 1, :] = jnp.sum(one, axis=0, keepdims=True)

    for kind, j, *step in sum_plan(g.widths, g.nz // 2, g.direct, g.early / g.slots):
        if kind == "make":
            make(j)
        elif kind == "near":
            send_back(j, early_rows, back_recv.at[j])
        elif kind == "combine":
            combine(j)
            if j in g.direct:
                rs_direct(j, far_away, 0)
            else:
                rs_step(j, 1, False)
        elif kind == "add":
            rs_step(j, step[0] + 1, False)
        elif kind == "close":
            combine_near(j)
            if j in g.direct:
                rs_direct(j, (1, g.nz - 1), 1)
            else:
                rs_step(j, 0, True)
        else:
            rs_last(j)

    def gone(ref, sem):
        pltpu.make_async_copy(ref, ref, sem).wait()

    some = pl.ds(0, g.nz - 1)
    gone(rawall.at[some], raw_send)
    gone(xall.at[some], z_send)
    for j in range(g.nj):
        gone(rsend[j], rs_send.at[j])

    @pl.when(parity == c)
    def _():
        fewer = pl.ds(0, g.xy - 1)
        gone(sbuf.at[fewer], xy_send)
        for j in range(g.nj):
            gone(back[j].at[fewer], ret_send.at[j])

    @pl.when(parity != c)
    def _():
        gone(sbuf, xy_send)
        for j in range(g.nj):
            gone(back[j], ret_send.at[j])

    half = out_ref.at[:, pl.ds(0, g.dh)]
    gone(half, out_send)
    gone(half, out_recv)


def scratch(g):
    dma = pltpu.SemaphoreType.DMA
    half = g.nz // 2
    vm = pltpu.VMEM
    return [
        vm((g.top, g.tok), jnp.int32),
        vm((g.top, g.tok), F32),
        vm((g.nz, g.tok, g.dim), BF16),
        vm((g.nz, 2 * g.top, LANES), F32),
        vm((g.xy * g.early, g.reach * g.tok), BF16),
        vm((g.xy * (g.slots - g.early), g.col - (g.reach - 1) * g.tok), BF16),
        vm((g.all_slots, g.col), BF16),
        vm((g.all_slots, g.col), BF16),
        vm((g.col, g.all_slots), BF16),
        vm((g.reach * g.tok, g.xy * g.early), BF16),
        vm((g.col - (g.reach - 1) * g.tok, g.xy * (g.slots - g.early)), BF16),
        vm((g.xy, g.slots, g.dim), BF16),
        vm((2, g.src, g.slots, g.dim), BF16),
        vm((g.dim, g.ff), BF16),
        vm((g.dim, g.ff), BF16),
        vm((g.ff, g.dim), BF16),
        vm((g.rows, g.ff), F32),
        vm((g.rows, g.ff), F32),
        vm((g.rows, g.ff), F32),
        vm((g.rows, g.ff), BF16),
        vm((g.rows, g.ff), BF16),
        dma((2,)),
        dma(()),
        dma((3,)),
        dma((3,)),
        dma((3,)),
        dma(()),
        dma(()),
        dma(()),
        dma((g.nq, 2, half)),
        dma(()),
        dma((2, len(g.near))),
        dma((2, g.nq)),
        dma((g.nj,)),
        dma((g.nj,)),
        dma((g.nj,)),
        dma((g.nj,)),
        dma((g.nj, g.nz - 1)),
        dma(()),
        dma(()),
        *[vm((2 if j else 1, g.src, g.slots if j else 16, w), BF16) for j, w in enumerate(g.widths)],
        *[vm((g.xy, g.slots if j else 16, w), BF16) for j, w in enumerate(g.widths)],
        *[vm((g.col, w), F32) for w in g.widths],
        *[vm((g.nz - 1, g.tok, w), BF16) for w in g.widths],
        *[vm((g.nz - 1, g.tok, w), BF16) for w in g.widths],
    ]


def per_device(ny, nz, nx, ahead, near, widths, direct, tokens, cotangent, expert_ids, gate_weights, w_gate, w_up, w_down):
    tok, dim = tokens.shape
    top = expert_ids.shape[1]
    g = Sizes(tok, dim, w_gate.shape[2], top, ny, nz, nx, ahead, near, widths, direct)
    vmem = pl.BlockSpec(memory_space=pltpu.VMEM)
    hbm = pl.BlockSpec(memory_space=pl.ANY)
    input_grad, gate_grad = pl.pallas_call(
        functools.partial(kernel, g),
        out_shape=(
            pltpu.VMEM((tok, dim), BF16),
            pltpu.VMEM((top, tok), F32),
        ),
        in_specs=[hbm] * 7,
        out_specs=(vmem, vmem),
        scratch_shapes=scratch(g),
        compiler_params=pltpu.CompilerParams(
            collective_id=0, has_side_effects=True, vmem_limit_bytes=60 * 1024 * 1024
        ),
    )(expert_ids.T, gate_weights.T, tokens, cotangent, w_gate, w_up, w_down)
    return input_grad, gate_grad.T.astype(BF16)


def solution(mesh, ny=NY, nz=NZ, nx=NX, ahead=(256,) * 8, near=((0,), (1,), (2, 3), (4, 5), (6, 7)), widths=(LANES, 256, 256, 256, 256), direct=()):
    placed = (
        P("expert", None),
        P("expert", None),
        P("expert", None),
        P("expert", None),
        P("expert", None, "half"),
        P("expert", None, "half"),
        P("expert", "half", None),
    )
    return jax.shard_map(
        functools.partial(per_device, ny, nz, nx, ahead, near, widths, direct),
        mesh=mesh,
        in_specs=placed,
        out_specs=(P("expert", None), P("expert", None)),
        check_vma=False,
    )
```

```python
import functools

import jax
import jax.numpy as jnp
from jax import lax
from jax.experimental import pallas as pl
from jax.experimental.pallas import tpu as pltpu
from jax.sharding import PartitionSpec as P

MESH = pl.DeviceIdType.MESH
F32 = jnp.float32
BF16 = jnp.bfloat16
NY, NZ, NX = 4, 8, 4
CAP = 6
LANES = 128


def nt(a, b):
    return lax.dot_general(a, b, (((1,), (1,)), ((), ())), preferred_element_type=F32)


def nn(a, b):
    return jnp.dot(a, b, preferred_element_type=F32)


class Sizes:
    def at(self, away):
        return self.order.index(away % self.nz)

    def __init__(self, tok, dim, half_ff, top, ny, nz, nx, ahead, near, widths):
        self.tok, self.dim, self.hf, self.ff, self.top = tok, dim, half_ff, 2 * half_ff, top
        self.ny, self.nz, self.nx = ny, nz, nx
        self.ahead = ahead
        self.starts = [sum(ahead[:q]) for q in range(len(ahead))]
        self.nq = len(ahead)
        self.near = near
        self.order = [0] + [v for k in range(1, nz // 2) for v in (k, nz - k)] + [nz // 2]
        self.early = 16
        self.reach = 3
        self.tiers = [
            (low, low + 16, low // CAP, (low + 15) // CAP + 1) for low in range(0, CAP * nz, 16)
        ]
        self.xy = ny * nx
        self.src = self.xy // 2
        self.slots = CAP * nz
        self.rows = self.src * self.slots
        self.all_slots = self.xy * self.slots
        self.col = nz * tok
        self.dh = dim // 2
        self.widths = widths
        self.cuts = [sum(widths[1:j]) for j in range(len(widths))]
        self.nj = len(widths)


def hops_of(number, way, half):
    return half if (number + way) % 2 == 0 else half - 1


def ring_plan(widths, near, half):
    lag, per_lane, hop = 2.3, 0.0036, 2.9
    size = [0.0]
    for w in widths:
        size.append(size[-1] + w / sum(widths))
    sends, came = [], {}
    for way in range(2):
        ready = {(q, 1): 0.0 for q in range(len(widths))}
        link = 0.0
        while ready:
            def due(item):
                q, step = item
                last = 15.5 + 23.0 * size[q] - hop * (hops_of(q, way, half) - step)
                return min(last, 4.0 + 11.4 * size[q]) if step == 1 else last

            now = max(link, min(ready.values()))
            q, step = min((item for item in ready if ready[item] <= now), key=due)
            del ready[q, step]
            sends.append((now, 0, "send", q, way, step))
            link = now + per_lane * widths[q]
            came[q, way, step] = link + lag
            if step < hops_of(q, way, half):
                ready[q, step + 1] = link + lag
    events = [(2.9, 1, "tables"), (6.6, 1, "tables_far")]
    first = [max(came[q, way, 1] for q in group for way in range(2)) for group in near]
    events += [(max(3.1, t), 2, "near", n) for n, t in enumerate(first)]
    latest = max(6.7, max(first))
    for q in range(len(widths)):
        t = max(v for k, v in came.items() if k[0] == q)
        events.append((max(t, latest + 0.01), 3, "far", q))
    return [event[2:] for event in sorted(sends + events)]


def sum_plan(widths, half):
    count = len(widths)
    plan, events, here, link = [], [], {}, 0.0
    clock = [0.0, 0.0]

    def issue(kind, j, cost, arrival, lanes):
        plan.append((kind, j))
        clock[0] += cost
        clock[1] = max(clock) + 0.0168 * lanes
        here[arrival, j] = clock[1] + 3.8

    for j in [1, 0, *range(2, count)]:
        issue("make", j, 1.8 if j else 0.4, "combine", widths[j] / 3)
        if j == 1:
            issue("middle", 1, 0.4, "mid", widths[1] / 3)
    for j in range(2, count):
        issue("middle", j, 0.4, "mid", widths[j] / 3)
    for j in range(1, count):
        issue("near", j, 0.4, "close", widths[j] / 3)
    events = [(here["combine", j], "combine", j, 0) for j in range(count)]
    now = clock[0]
    while events:
        at, kind, j, step = min(events)
        events.remove((at, kind, j, step))
        now = max(now, at)
        plan.append((kind, j, step))
        now += {"combine": 0.4, "mid": 0.5, "add": 0.25, "close": 0.6, "last": 0.3}[kind]
        if kind == "last":
            continue
        link = max(link, now) + 0.0036 * widths[j]
        there = link + 2.3
        if kind == "close" or (j == 0 and step == half - 1):
            events.append((there, "last", j, 0))
        elif j == 0:
            events.append((there, "add", j, step + 1))
        else:
            after = {"combine": "mid", "mid": "add", "add": "close"}[kind]
            events.append((max(there, here.get((after, j), 0.0)), after, j, 0))
    return plan


def kernel(
    g, ids_hbm, gates_hbm, tok_hbm, cot_hbm, wg_hbm, wu_hbm, wd_hbm, out_ref, gate_ref,
    ids_ref, gates_ref, xall, rawall, pick_near, pick_far, pick, scaled, pick_t, near_t, mid_t, far_t, sbuf, rbuf, wg, wu, wd, gacc, uacc, hacc, gg, gu,
    table_sem, own_sem, w_own_sem, w_send, w_recv, raw_send, raw_recv, z_send, z_recv, xy_send, near_recv, xy_recv,
    ret_send, ret_recv, mid_recv, back_recv, rs_send, rs_recv, out_send, out_recv, *lists,
):
    ret, back, part, rsend, rrecv = (lists[k * g.nj:(k + 1) * g.nj] for k in range(5))
    e = lax.axis_index("expert")
    c = lax.axis_index("half")
    x = lax.rem(e, g.nx)
    z = lax.rem(e // g.nx, g.nz)
    y = e // (g.nx * g.nz)
    other = 1 - c
    parity = lax.rem(x + y, 2)

    def chip(yy, zz, xx):
        return (yy * g.nz + zz) * g.nx + xx

    def zmod(v):
        return lax.rem(v + 2 * g.nz, g.nz)

    tables_in = (
        pltpu.make_async_copy(ids_hbm, ids_ref, table_sem.at[0]),
        pltpu.make_async_copy(gates_hbm, gates_ref, table_sem.at[1]),
    )
    for copy in tables_in:
        copy.start()

    @pl.when(c == 0)
    def _():
        pltpu.make_async_copy(tok_hbm, xall.at[0], own_sem).start()

    @pl.when(c == 1)
    def _():
        pltpu.make_async_copy(cot_hbm, xall.at[0], own_sem).start()

    cut = pl.ds(pl.multiple_of(c * g.hf, LANES), g.hf)
    places = (wg.at[:, cut], wu.at[:, cut], wd.at[cut, :])
    weights = (wg_hbm.at[0], wu_hbm.at[0], wd_hbm.at[0])

    def weight_own(i):
        return pltpu.make_async_copy(weights[i], places[i], w_own_sem.at[i])

    def weight_swap(i):
        return pltpu.make_async_remote_copy(
            places[i], places[i], w_send.at[i], w_recv.at[i], device_id=(e, other), device_id_type=MESH
        )

    barrier = pltpu.get_barrier_semaphore()
    for dz in range(1, g.nz):
        pl.semaphore_signal(barrier, inc=1, device_id=(chip(y, zmod(z + dz), x), c), device_id_type=MESH)
    for dy in range(g.ny):
        for dx in range(g.nx):
            peer = chip(lax.rem(y + dy, g.ny), z, lax.rem(x + dx, g.nx))
            if dy or dx:
                pl.semaphore_signal(barrier, inc=1, device_id=(peer, c), device_id_type=MESH)
            pl.semaphore_signal(barrier, inc=1, device_id=(peer, other), device_id_type=MESH)
    for i in range(3):
        weight_own(i).start()
    for copy in tables_in:
        copy.wait()
    table = jnp.concatenate([ids_ref[...].astype(F32), gates_ref[...]], axis=0)
    rawall[0] = jnp.concatenate([table, table], axis=1)
    pl.semaphore_wait(barrier, 2 * g.xy - 1 + g.nz - 1)

    def raw_copy(dz):
        return pltpu.make_async_remote_copy(
            rawall.at[0], rawall.at[g.at(-dz)], raw_send, raw_recv.at[g.at(-dz) // 4],
            device_id=(chip(y, zmod(z + dz), x), c), device_id_type=MESH,
        )

    for dz in sorted(range(1, g.nz), key=lambda v: g.at(-v)):
        raw_copy(dz).start()

    def hops(number, way):
        return hops_of(number, way, g.nz // 2)

    def lanes(q):
        return pl.ds(g.starts[q], g.ahead[q])

    def z_copy(q, way, step):
        sign = 1 - 2 * way
        src = xall.at[g.at(-sign * (step - 1)), :, lanes(q)]
        dst = xall.at[g.at(-sign * step), :, lanes(q)]
        return pltpu.make_async_remote_copy(
            src, dst, z_send, z_recv.at[q, way, step - 1],
            device_id=(chip(y, zmod(z + sign), x), c), device_id_type=MESH,
        )

    pltpu.make_async_copy(tok_hbm, xall.at[0], own_sem).wait()

    def keys(count):
        lane = lax.broadcasted_iota(jnp.int32, (2 * g.top, LANES), 1)
        pairs = [jnp.where(lane < g.tok, rawall[2 * p], rawall[2 * p + 1]) for p in range(count // 2)]
        raw = jnp.concatenate(pairs, axis=1)
        col = count * g.tok
        place = lax.broadcasted_iota(jnp.int32, (g.xy, col), 0)
        named_by = (((place // g.nx) * g.nz + z) * g.nx + lax.rem(place, g.nx)).astype(F32)
        named = jnp.zeros((g.xy, col), F32)
        weight = jnp.zeros((g.xy, col), F32)
        for k in range(g.top):
            hit = raw[k:k + 1, :] == named_by
            named = named + jnp.where(hit, 1.0, 0.0)
            weight = weight + jnp.where(hit, raw[g.top + k:g.top + k + 1, :], 0.0)
        early = lax.broadcasted_iota(jnp.int32, (col, col), 0)
        late = lax.broadcasted_iota(jnp.int32, (col, col), 1)
        before = jnp.where((early // g.tok == late // g.tok) & (early < late), 1.0, 0.0).astype(BF16)
        rank = nn(named.astype(BF16), before)
        token = lax.broadcasted_iota(jnp.int32, (g.xy, col), 1)
        return jnp.where(named > 0.0, rank + (CAP * (token // g.tok)).astype(F32), -1.0), weight

    def tables():
        came = rawall.at[pl.ds(1, 3)]
        pltpu.make_async_copy(came, came, raw_recv.at[0]).wait()
        key, _ = keys(4)
        width = g.reach * g.tok
        slot = lax.broadcasted_iota(jnp.int32, (g.early, width), 0).astype(F32)
        for d in range(g.xy):
            hit = key[d:d + 1, :width] == slot
            pick_near[d * g.early:(d + 1) * g.early, :] = jnp.where(hit, 1.0, 0.0).astype(BF16)

    def tables_far():
        came = rawall.at[pl.ds(4, g.nz - 4)]
        pltpu.make_async_copy(came, came, raw_recv.at[1]).wait()
        key, weight = keys(g.nz)
        slot = lax.broadcasted_iota(jnp.int32, (g.slots, g.col), 0).astype(F32)
        for d in range(g.xy):
            hit = key[d:d + 1, :] == slot
            pick[d * g.slots:(d + 1) * g.slots, :] = jnp.where(hit, 1.0, 0.0).astype(BF16)
            scaled[d * g.slots:(d + 1) * g.slots, :] = jnp.where(hit, weight[d:d + 1, :], 0.0).astype(BF16)
        late_slots = g.slots - g.early
        late = pick[...].reshape(g.xy, g.slots, g.col)[:, g.early:, (g.reach - 1) * g.tok:]
        pick_far[...] = late.reshape(g.xy * late_slots, g.col - (g.reach - 1) * g.tok)

    mine = y * (g.nx // 2) + x // 2

    def to_plane(rows, span, sem, off):
        yy = lax.rem(y + off // g.nx, g.ny)
        xx = lax.rem(x + lax.rem(off, g.nx), g.nx)
        src = sbuf.at[yy * g.nx + xx, rows, span]
        dst = rbuf.at[c, mine, rows, span]
        stays = (off == 0) & (parity == c)

        @pl.when(jnp.logical_not(stays))
        def _():
            pltpu.make_async_remote_copy(
                src, dst, xy_send, sem, device_id=(chip(yy, z, xx), parity), device_id_type=MESH
            ).start()

        @pl.when(stays)
        def _():
            pltpu.make_async_copy(src, dst, sem).start()

    early_rows, late_rows = pl.ds(0, g.early), pl.ds(g.early, g.slots - g.early)

    def near_span(n):
        return g.starts[g.near[n][0]], sum(g.ahead[q] for q in g.near[n])

    def gather_near(n):
        start, width = near_span(n)
        rows = xall[:g.reach, :, start:start + width].reshape(g.reach * g.tok, width)
        got = nn(pick_near[...], rows).astype(BF16)
        sbuf[:, :g.early, start:start + width] = got.reshape(g.xy, g.early, width)

        @pl.loop(0, g.xy)
        def _(off):
            to_plane(early_rows, pl.ds(start, width), near_recv.at[c, n], off)

    def gather_far(q):
        start, width = g.starts[q], g.ahead[q]
        rows = xall[g.reach - 1:, :, start:start + width].reshape(g.col - (g.reach - 1) * g.tok, width)
        groups = 4
        per = g.xy // groups
        late = g.slots - g.early
        for i in range(groups):
            got = nn(pick_far[i * per * late:(i + 1) * per * late, :], rows).astype(BF16)
            sbuf[i * per:(i + 1) * per, g.early:, start:start + width] = got.reshape(per, late, width)

        @pl.loop(0, g.xy)
        def _(off):
            to_plane(late_rows, pl.ds(start, width), xy_recv.at[c, q], off)

    arrived = set()

    def need(q, steps):
        for at in steps:
            for way in range(2):
                if at <= hops(q, way) and (q, way, at) not in arrived:
                    arrived.add((q, way, at))
                    z_copy(q, way, at).wait_recv()

    def need_one(q, way, at):
        if at and (q, way, at) not in arrived:
            arrived.add((q, way, at))
            z_copy(q, way, at).wait_recv()

    swapped = False
    for step in ring_plan(g.ahead, g.near, g.nz // 2):
        if step[0] == "send":
            _, q, way, at = step
            need_one(q, way, at - 1)
            z_copy(q, way, at).start()
        elif step[0] == "tables":
            tables()
        elif step[0] == "tables_far":
            tables_far()
        elif step[0] == "near":
            for q in g.near[step[1]]:
                need(q, (1,))
            gather_near(step[1])
            if not swapped:
                swapped = True
                for i in range(3):
                    weight_own(i).wait()
                    weight_swap(i).start()
        else:
            need(step[1], range(1, g.nz // 2 + 1))
            gather_far(step[1])

    early = lax.broadcasted_iota(jnp.int32, (g.col, g.col), 0)
    late = lax.broadcasted_iota(jnp.int32, (g.col, g.col), 1)
    same = jnp.where(early == late, 1.0, 0.0).astype(BF16)
    pick_t[...] = nt(same, pick[...]).astype(BF16)
    whole = scaled[...].reshape(g.xy, g.slots, g.col)
    for ref, (low, high, first, last) in ((near_t, g.tiers[0]), (mid_t, g.tiers[1]), (far_t, g.tiers[2])):
        cols = (last - first) * g.tok
        rows = whole[:, low:high, first * g.tok:last * g.tok].reshape(g.xy * (high - low), cols)
        ref[...] = nt(same[:cols, :cols], rows).astype(BF16)

    for i in range(3):
        weight_swap(i).wait()

    for q in range(g.nq):
        feats = slice(g.starts[q], g.starts[q] + g.ahead[q])
        for n, group in enumerate(g.near):
            if q == group[0]:
                start, width = near_span(n)
                for kind in range(2):
                    came = rbuf.at[kind, :, early_rows, pl.ds(start, width)]
                    pltpu.make_async_copy(came, came, near_recv.at[kind, n]).wait()
        for kind in range(2):
            came = rbuf.at[kind, :, late_rows, lanes(q)]
            pltpu.make_async_copy(came, came, xy_recv.at[kind, q]).wait()
        rows = rbuf[0, :, :, feats].reshape(g.rows, g.ahead[q])
        grads = rbuf[1, :, :, feats].reshape(g.rows, g.ahead[q])
        if q == 0:
            gacc[...] = nn(rows, wg[feats, :])
            uacc[...] = nn(rows, wu[feats, :])
            hacc[...] = nt(grads, wd[:, feats])
        else:
            gacc[...] += nn(rows, wg[feats, :])
            uacc[...] += nn(rows, wu[feats, :])
            hacc[...] += nt(grads, wd[:, feats])

    for i in range(g.src):
        span = slice(i * g.slots, (i + 1) * g.slots)
        gate_pre, up_pre, grad_hidden = gacc[span, :], uacc[span, :], hacc[span, :]
        sigma = jax.nn.sigmoid(gate_pre)
        down = grad_hidden * (gate_pre * sigma)
        score = jnp.sum(down * up_pre, axis=1, keepdims=True)
        wide = jnp.broadcast_to(score, (g.slots, LANES)).astype(BF16)
        first = jnp.where(lax.broadcasted_iota(jnp.int32, (16, LANES), 1) == 0, 1.0, 0.0).astype(BF16)
        ret[0][0, i, :, :g.slots] = nt(first, wide).astype(BF16)
        gu[span, :] = down.astype(BF16)
        gg[span, :] = (grad_hidden * up_pre * sigma * (1.0 + gate_pre * (1.0 - sigma))).astype(BF16)

    here_d = y * g.nx + x

    def to_source(j, h, i, rows, sem):
        dy = i // (g.nx // 2)
        dx = 2 * lax.rem(i, g.nx // 2) + lax.rem(dy + parity + c, 2)
        yy = lax.rem(y + dy, g.ny)
        xx = lax.rem(x + dx, g.nx)
        src = ret[j].at[h if j else 0, yy * (g.nx // 2) + xx // 2, rows]
        dst = back[j].at[here_d, rows]
        stays = (xx == x) & (yy == y) & (c == h)

        @pl.when(jnp.logical_not(stays))
        def _():
            pltpu.make_async_remote_copy(
                src, dst, ret_send.at[j], sem, device_id=(chip(yy, z, xx), h), device_id_type=MESH
            ).start()

        @pl.when(stays)
        def _():
            pltpu.make_async_copy(src, dst, sem).start()

    def tier_rows(n):
        return pl.ds(g.tiers[n][0], g.tiers[n][1] - g.tiers[n][0])

    def send_back(j, rows, sem):
        @pl.loop(0, g.src)
        def _(i):
            for h in range(2):
                to_source(j, h, i, rows, sem)

    def make(j):
        w = g.widths[j]
        if j:
            cuts = [h * g.dh + g.cuts[j] for h in range(2)]
            both = [jnp.concatenate([ref[cut:cut + w, :] for cut in cuts], axis=0) for ref in (wg, wu)]
            got = (nt(gg[...], both[0]) + nt(gu[...], both[1])).astype(BF16)
            for h in range(2):
                ret[j][h] = got[:, h * w:(h + 1) * w].reshape(g.src, g.slots, w)

        send_back(j, tier_rows(2) if j else pl.ds(0, 16), ret_recv.at[j])

    def combine(j):
        came = back[j].at[:, tier_rows(2) if j else pl.ds(0, 16)]
        pltpu.make_async_copy(came, came, ret_recv.at[j]).wait()
        if j == 0:
            slot = lax.broadcasted_iota(jnp.int32, (g.slots, g.slots), 0)
            same = jnp.where(slot == lax.broadcasted_iota(jnp.int32, (g.slots, g.slots), 1), 1.0, 0.0).astype(BF16)
            at = lax.broadcasted_iota(jnp.int32, (g.slots, LANES), 1)
            placed = []
            for d in range(g.xy):
                column = nt(same, back[0][d, :, :g.slots])[:, :1]
                expert = ((d // g.nx) * g.nz + z) * g.nx + d % g.nx
                placed.append(jnp.where(at == expert, column, 0.0).astype(BF16))
            part[0][...] = nn(pick_t[...], jnp.concatenate(placed, axis=0))
        else:
            got, first, _ = tier_sum(j, far_t, 2)
            part[j][first * g.tok:, :] = got

    def tier_sum(j, weights, n):
        low, high, first, last = g.tiers[n]
        rows = back[j][:, low:high, :].reshape(g.xy * (high - low), g.widths[j])
        return nn(weights[...], rows), first, last

    def combine_more(j, weights, n, sem):
        came = back[j].at[:, tier_rows(n)]
        pltpu.make_async_copy(came, came, sem).wait()
        got, first, last = tier_sum(j, weights, n)
        edge = (last - 1 - first) * g.tok
        part[j][first * g.tok:(last - 1) * g.tok, :] = got[:edge]
        part[j][(last - 1) * g.tok:last * g.tok, :] += got[edge:]

    def own_part(j, away):
        block = g.at(away)
        return part[j][block * g.tok:(block + 1) * g.tok, :]

    def spot(j, way, step):
        return step - 1 + way * hops(j, 0)

    def rs_copy(j, way, step):
        sign = 1 - 2 * way
        n = spot(j, way, step)
        return pltpu.make_async_remote_copy(
            rsend[j].at[n], rrecv[j].at[n], rs_send.at[j], rs_recv.at[j, n],
            device_id=(chip(y, zmod(z + sign), x), c), device_id_type=MESH,
        )

    passed = {}

    def rs_next(j, way):
        n = hops(j, way)
        at = passed.get((j, way), 0) + 1
        passed[j, way] = at
        sign = 1 - 2 * way
        term = own_part(j, sign * (n + 1 - at))
        if at > 1:
            rs_copy(j, way, at - 1).wait_recv()
            term = term + rrecv[j][spot(j, way, at - 1)].astype(F32)
        rsend[j][spot(j, way, at)] = term.astype(BF16)
        rs_copy(j, way, at).start()

    def rs_move(j, kind):
        for way in range(2):
            n, done = hops(j, way), passed.get((j, way), 0)
            if j == 0:
                go = done < n
            elif kind == "combine":
                go = g.at((1 - 2 * way) * n) >= g.tiers[1][3]
            elif kind == "add":
                go = done < n - 1
            else:
                go = True
            if go:
                rs_next(j, way)

    def swap(j):
        span = pl.ds(pl.multiple_of(c * g.dh + g.cuts[j], LANES), g.widths[j])
        return pltpu.make_async_remote_copy(
            out_ref.at[:, span], out_ref.at[:, span], out_send, out_recv,
            device_id=(e, other), device_id_type=MESH,
        )

    def rs_last(j):
        total = own_part(j, 0)
        for way in range(2):
            rs_copy(j, way, hops(j, way)).wait_recv()
            total = total + rrecv[j][spot(j, way, hops(j, way))].astype(F32)
        if j:
            out_ref[:, pl.ds(pl.multiple_of(c * g.dh + g.cuts[j], LANES), g.widths[j])] = total.astype(BF16)
            swap(j).start()
        else:
            square = (LANES, LANES)
            same = lax.broadcasted_iota(jnp.int32, square, 0) == lax.broadcasted_iota(jnp.int32, square, 1)
            scores = nt(jnp.where(same, 1.0, 0.0).astype(BF16), total.astype(BF16))
            expert_at = lax.broadcasted_iota(jnp.int32, (LANES, g.tok), 0)
            for k in range(g.top):
                one = jnp.where(expert_at == ids_ref[k:k + 1, :], scores, 0.0)
                gate_ref[k:k + 1, :] = jnp.sum(one, axis=0, keepdims=True)

    for kind, j, *_ in sum_plan(g.widths, g.nz // 2):
        if kind == "make":
            make(j)
        elif kind == "middle":
            send_back(j, tier_rows(1), mid_recv.at[j])
        elif kind == "near":
            send_back(j, tier_rows(0), back_recv.at[j])
        elif kind == "last":
            rs_last(j)
        else:
            if kind == "combine":
                combine(j)
            elif kind == "mid":
                combine_more(j, mid_t, 1, mid_recv.at[j])
            elif kind == "close":
                combine_more(j, near_t, 0, back_recv.at[j])
            rs_move(j, kind)

    def gone(ref, sem):
        pltpu.make_async_copy(ref, ref, sem).wait()

    some = pl.ds(0, g.nz - 1)
    gone(rawall.at[some], raw_send)
    gone(xall.at[some], z_send)
    for j in range(g.nj):
        gone(rsend[j], rs_send.at[j])

    @pl.when(parity == c)
    def _():
        fewer = pl.ds(0, g.xy - 1)
        gone(sbuf.at[fewer], xy_send)
        for j in range(g.nj):
            gone(back[j].at[fewer], ret_send.at[j])

    @pl.when(parity != c)
    def _():
        gone(sbuf, xy_send)
        for j in range(g.nj):
            gone(back[j], ret_send.at[j])

    half = out_ref.at[:, pl.ds(0, g.dh)]
    gone(half, out_send)
    gone(half, out_recv)


def scratch(g):
    dma = pltpu.SemaphoreType.DMA
    half = g.nz // 2
    vm = pltpu.VMEM
    return [
        vm((g.top, g.tok), jnp.int32),
        vm((g.top, g.tok), F32),
        vm((g.nz, g.tok, g.dim), BF16),
        vm((g.nz, 2 * g.top, LANES), F32),
        vm((g.xy * g.early, g.reach * g.tok), BF16),
        vm((g.xy * (g.slots - g.early), g.col - (g.reach - 1) * g.tok), BF16),
        vm((g.all_slots, g.col), BF16),
        vm((g.all_slots, g.col), BF16),
        vm((g.col, g.all_slots), BF16),
        *[vm(((last - first) * g.tok, g.xy * (high - low)), BF16) for low, high, first, last in g.tiers],
        vm((g.xy, g.slots, g.dim), BF16),
        vm((2, g.src, g.slots, g.dim), BF16),
        vm((g.dim, g.ff), BF16),
        vm((g.dim, g.ff), BF16),
        vm((g.ff, g.dim), BF16),
        vm((g.rows, g.ff), F32),
        vm((g.rows, g.ff), F32),
        vm((g.rows, g.ff), F32),
        vm((g.rows, g.ff), BF16),
        vm((g.rows, g.ff), BF16),
        dma((2,)),
        dma(()),
        dma((3,)),
        dma((3,)),
        dma((3,)),
        dma(()),
        dma((2,)),
        dma(()),
        dma((g.nq, 2, half)),
        dma(()),
        dma((2, len(g.near))),
        dma((2, g.nq)),
        dma((g.nj,)),
        dma((g.nj,)),
        dma((g.nj,)),
        dma((g.nj,)),
        dma((g.nj,)),
        dma((g.nj, g.nz - 1)),
        dma(()),
        dma(()),
        *[vm((2 if j else 1, g.src, g.slots if j else 16, w), BF16) for j, w in enumerate(g.widths)],
        *[vm((g.xy, g.slots if j else 16, w), BF16) for j, w in enumerate(g.widths)],
        *[vm((g.col, w), F32) for w in g.widths],
        *[vm((g.nz - 1, g.tok, w), BF16) for w in g.widths],
        *[vm((g.nz - 1, g.tok, w), BF16) for w in g.widths],
    ]


def per_device(ny, nz, nx, ahead, near, widths, tokens, cotangent, expert_ids, gate_weights, w_gate, w_up, w_down):
    tok, dim = tokens.shape
    top = expert_ids.shape[1]
    g = Sizes(tok, dim, w_gate.shape[2], top, ny, nz, nx, ahead, near, widths)
    vmem = pl.BlockSpec(memory_space=pltpu.VMEM)
    hbm = pl.BlockSpec(memory_space=pl.ANY)
    input_grad, gate_grad = pl.pallas_call(
        functools.partial(kernel, g),
        out_shape=(
            pltpu.VMEM((tok, dim), BF16),
            pltpu.VMEM((top, tok), F32),
        ),
        in_specs=[hbm] * 7,
        out_specs=(vmem, vmem),
        scratch_shapes=scratch(g),
        compiler_params=pltpu.CompilerParams(
            collective_id=0, has_side_effects=True, vmem_limit_bytes=60 * 1024 * 1024
        ),
    )(expert_ids.T, gate_weights.T, tokens, cotangent, w_gate, w_up, w_down)
    return input_grad, gate_grad.T.astype(BF16)


def solution(mesh, ny=NY, nz=NZ, nx=NX, ahead=(256,) * 8, near=((0,), (1,), (2, 3), (4, 5), (6, 7)), widths=(LANES, 256, 256, 256, 256)):
    placed = (
        P("expert", None),
        P("expert", None),
        P("expert", None),
        P("expert", None),
        P("expert", None, "half"),
        P("expert", None, "half"),
        P("expert", "half", None),
    )
    return jax.shard_map(
        functools.partial(per_device, ny, nz, nx, ahead, near, widths),
        mesh=mesh,
        in_specs=placed,
        out_specs=(P("expert", None), P("expert", None)),
        check_vma=False,
    )
```

```python
import functools

import jax
import jax.numpy as jnp
from jax import lax
from jax.experimental import pallas as pl
from jax.experimental.pallas import tpu as pltpu
from jax.sharding import PartitionSpec as P

MESH = pl.DeviceIdType.MESH
F32 = jnp.float32
BF16 = jnp.bfloat16
NY, NZ, NX = 4, 8, 4
CAP = 6
LANES = 128


def nt(a, b):
    return lax.dot_general(a, b, (((1,), (1,)), ((), ())), preferred_element_type=F32)


def nn(a, b):
    return jnp.dot(a, b, preferred_element_type=F32)


class Sizes:
    def at(self, away):
        return self.order.index(away % self.nz)

    def __init__(self, tok, dim, half_ff, top, ny, nz, nx, ahead, near, widths):
        self.tok, self.dim, self.hf, self.ff, self.top = tok, dim, half_ff, 2 * half_ff, top
        self.ny, self.nz, self.nx = ny, nz, nx
        self.ahead = ahead
        self.starts = [sum(ahead[:q]) for q in range(len(ahead))]
        self.nq = len(ahead)
        self.near = near
        self.order = [0] + [v for k in range(1, nz // 2) for v in (k, nz - k)] + [nz // 2]
        self.early = 16
        self.reach = 3
        self.tiers = [
            (low, low + 16, low // CAP, (low + 15) // CAP + 1) for low in range(0, CAP * nz, 16)
        ]
        self.xy = ny * nx
        self.src = self.xy // 2
        self.slots = CAP * nz
        self.rows = self.src * self.slots
        self.all_slots = self.xy * self.slots
        self.col = nz * tok
        self.dh = dim // 2
        self.widths = widths
        self.cuts = [sum(widths[1:j]) for j in range(len(widths))]
        self.nj = len(widths)


def hops_of(number, way, half):
    return half if (number + way) % 2 == 0 else half - 1


def ring_plan(widths, near, half):
    lag, per_lane, hop = 2.3, 0.0036, 2.9
    size = [0.0]
    for w in widths:
        size.append(size[-1] + w / sum(widths))
    sends, came = [], {}
    for way in range(2):
        ready = {(q, 1): 0.0 for q in range(len(widths))}
        link = 0.0
        while ready:
            def due(item):
                q, step = item
                last = 15.5 + 23.0 * size[q] - hop * (hops_of(q, way, half) - step)
                return min(last, 4.0 + 11.4 * size[q]) if step == 1 else last

            now = max(link, min(ready.values()))
            q, step = min((item for item in ready if ready[item] <= now), key=due)
            del ready[q, step]
            sends.append((now, 0, "send", q, way, step))
            link = now + per_lane * widths[q]
            came[q, way, step] = link + lag
            if step < hops_of(q, way, half):
                ready[q, step + 1] = link + lag
    events = [(2.9, 1, "tables"), (6.6, 1, "tables_far")]
    first = [max(came[q, way, 1] for q in group for way in range(2)) for group in near]
    events += [(max(3.1, t), 2, "near", n) for n, t in enumerate(first)]
    latest = max(6.7, max(first))
    for q in range(len(widths)):
        t = max(v for k, v in came.items() if k[0] == q)
        events.append((max(t, latest + 0.01), 3, "far", q))
    return [event[2:] for event in sorted(sends + events)]


def sum_plan(widths, half):
    count = len(widths)
    plan, events, here, link = [], [], {}, 0.0
    clock = [0.0, 0.0]

    def issue(kind, j, cost, arrival, lanes):
        plan.append((kind, j))
        clock[0] += cost
        clock[1] = max(clock) + 0.0168 * lanes
        here[arrival, j] = clock[1] + 3.8

    for j in [1, 0, *range(2, count)]:
        issue("make", j, 1.8 if j else 0.4, "combine", widths[j] / 3)
        if j == 1:
            issue("middle", 1, 0.4, "mid", widths[1] / 3)
    for j in range(2, count):
        issue("middle", j, 0.4, "mid", widths[j] / 3)
    for j in range(1, count):
        issue("near", j, 0.4, "close", widths[j] / 3)
    events = [(here["combine", j], "combine", j, 0) for j in range(count)]
    now = clock[0]
    while events:
        at, kind, j, step = min(events)
        events.remove((at, kind, j, step))
        now = max(now, at)
        plan.append((kind, j, step))
        now += {"combine": 0.4, "mid": 0.5, "add": 0.25, "close": 0.6, "last": 0.3}[kind]
        if kind == "last":
            continue
        link = max(link, now) + 0.0036 * widths[j]
        there = link + 2.3
        if kind == "close" or (j == 0 and step == half - 1):
            events.append((there, "last", j, 0))
        elif j == 0:
            events.append((there, "add", j, step + 1))
        else:
            after = {"combine": "mid", "mid": "add", "add": "close"}[kind]
            events.append((max(there, here.get((after, j), 0.0)), after, j, 0))
    return plan


def kernel(
    g, ids_hbm, gates_hbm, tok_hbm, cot_hbm, wg_hbm, wu_hbm, wd_hbm, out_ref, gate_ref,
    ids_ref, gates_ref, xall, rawall, pick_near, pick_far, pick, scaled, pick_t, near_t, mid_t, far_t, sbuf, rbuf, wg, wu, wd, gacc, uacc, hacc, gg, gu,
    table_sem, own_sem, w_own_sem, w_send, w_recv, raw_send, raw_recv, z_send, z_recv, xy_send, near_recv, xy_recv,
    ret_send, ret_recv, mid_recv, back_recv, rs_send, rs_recv, out_send, out_recv, *lists,
):
    ret, back, part, rsend, rrecv = (lists[k * g.nj:(k + 1) * g.nj] for k in range(5))
    e = lax.axis_index("expert")
    c = lax.axis_index("half")
    x = lax.rem(e, g.nx)
    z = lax.rem(e // g.nx, g.nz)
    y = e // (g.nx * g.nz)
    other = 1 - c
    parity = lax.rem(x + y, 2)

    def chip(yy, zz, xx):
        return (yy * g.nz + zz) * g.nx + xx

    def zmod(v):
        return lax.rem(v + 2 * g.nz, g.nz)

    tables_in = (
        pltpu.make_async_copy(ids_hbm, ids_ref, table_sem.at[0]),
        pltpu.make_async_copy(gates_hbm, gates_ref, table_sem.at[1]),
    )
    for copy in tables_in:
        copy.start()

    @pl.when(c == 0)
    def _():
        pltpu.make_async_copy(tok_hbm, xall.at[0], own_sem).start()

    @pl.when(c == 1)
    def _():
        pltpu.make_async_copy(cot_hbm, xall.at[0], own_sem).start()

    cut = pl.ds(pl.multiple_of(c * g.hf, LANES), g.hf)
    places = (wg.at[:, cut], wu.at[:, cut], wd.at[cut, :])
    weights = (wg_hbm.at[0], wu_hbm.at[0], wd_hbm.at[0])

    def weight_own(i):
        return pltpu.make_async_copy(weights[i], places[i], w_own_sem.at[i])

    def weight_swap(i):
        return pltpu.make_async_remote_copy(
            places[i], places[i], w_send.at[i], w_recv.at[i], device_id=(e, other), device_id_type=MESH
        )

    barrier = pltpu.get_barrier_semaphore()
    for dz in range(1, g.nz):
        pl.semaphore_signal(barrier, inc=1, device_id=(chip(y, zmod(z + dz), x), c), device_id_type=MESH)
    for dy in range(g.ny):
        for dx in range(g.nx):
            peer = chip(lax.rem(y + dy, g.ny), z, lax.rem(x + dx, g.nx))
            if dy or dx:
                pl.semaphore_signal(barrier, inc=1, device_id=(peer, c), device_id_type=MESH)
            pl.semaphore_signal(barrier, inc=1, device_id=(peer, other), device_id_type=MESH)
    for i in range(3):
        weight_own(i).start()
    for copy in tables_in:
        copy.wait()
    table = jnp.concatenate([ids_ref[...].astype(F32), gates_ref[...]], axis=0)
    rawall[0] = jnp.concatenate([table, table], axis=1)
    pl.semaphore_wait(barrier, 2 * g.xy - 1 + g.nz - 1)

    def raw_copy(dz):
        return pltpu.make_async_remote_copy(
            rawall.at[0], rawall.at[g.at(-dz)], raw_send, raw_recv.at[g.at(-dz) // 4],
            device_id=(chip(y, zmod(z + dz), x), c), device_id_type=MESH,
        )

    for dz in sorted(range(1, g.nz), key=lambda v: g.at(-v)):
        raw_copy(dz).start()

    def hops(number, way):
        return hops_of(number, way, g.nz // 2)

    def lanes(q):
        return pl.ds(g.starts[q], g.ahead[q])

    def z_copy(q, way, step):
        sign = 1 - 2 * way
        src = xall.at[g.at(-sign * (step - 1)), :, lanes(q)]
        dst = xall.at[g.at(-sign * step), :, lanes(q)]
        return pltpu.make_async_remote_copy(
            src, dst, z_send, z_recv.at[q, way, step - 1],
            device_id=(chip(y, zmod(z + sign), x), c), device_id_type=MESH,
        )

    pltpu.make_async_copy(tok_hbm, xall.at[0], own_sem).wait()

    def keys(count):
        lane = lax.broadcasted_iota(jnp.int32, (2 * g.top, LANES), 1)
        pairs = [jnp.where(lane < g.tok, rawall[2 * p], rawall[2 * p + 1]) for p in range(count // 2)]
        raw = jnp.concatenate(pairs, axis=1)
        col = count * g.tok
        place = lax.broadcasted_iota(jnp.int32, (g.xy, col), 0)
        named_by = (((place // g.nx) * g.nz + z) * g.nx + lax.rem(place, g.nx)).astype(F32)
        named = jnp.zeros((g.xy, col), F32)
        weight = jnp.zeros((g.xy, col), F32)
        for k in range(g.top):
            hit = raw[k:k + 1, :] == named_by
            named = named + jnp.where(hit, 1.0, 0.0)
            weight = weight + jnp.where(hit, raw[g.top + k:g.top + k + 1, :], 0.0)
        early = lax.broadcasted_iota(jnp.int32, (col, col), 0)
        late = lax.broadcasted_iota(jnp.int32, (col, col), 1)
        before = jnp.where((early // g.tok == late // g.tok) & (early < late), 1.0, 0.0).astype(BF16)
        rank = nn(named.astype(BF16), before)
        token = lax.broadcasted_iota(jnp.int32, (g.xy, col), 1)
        return jnp.where(named > 0.0, rank + (CAP * (token // g.tok)).astype(F32), -1.0), weight

    def tables():
        came = rawall.at[pl.ds(1, 3)]
        pltpu.make_async_copy(came, came, raw_recv.at[0]).wait()
        key, _ = keys(4)
        width = g.reach * g.tok
        slot = lax.broadcasted_iota(jnp.int32, (g.early, width), 0).astype(F32)
        for d in range(g.xy):
            hit = key[d:d + 1, :width] == slot
            pick_near[d * g.early:(d + 1) * g.early, :] = jnp.where(hit, 1.0, 0.0).astype(BF16)

    def tables_far():
        came = rawall.at[pl.ds(4, g.nz - 4)]
        pltpu.make_async_copy(came, came, raw_recv.at[1]).wait()
        key, weight = keys(g.nz)
        slot = lax.broadcasted_iota(jnp.int32, (g.slots, g.col), 0).astype(F32)
        for d in range(g.xy):
            hit = key[d:d + 1, :] == slot
            pick[d * g.slots:(d + 1) * g.slots, :] = jnp.where(hit, 1.0, 0.0).astype(BF16)
            scaled[d * g.slots:(d + 1) * g.slots, :] = jnp.where(hit, weight[d:d + 1, :], 0.0).astype(BF16)
        late_slots = g.slots - g.early
        late = pick[...].reshape(g.xy, g.slots, g.col)[:, g.early:, (g.reach - 1) * g.tok:]
        pick_far[...] = late.reshape(g.xy * late_slots, g.col - (g.reach - 1) * g.tok)

    mine = y * (g.nx // 2) + x // 2

    def to_plane(rows, span, sem, off):
        yy = lax.rem(y + off // g.nx, g.ny)
        xx = lax.rem(x + lax.rem(off, g.nx), g.nx)
        src = sbuf.at[yy * g.nx + xx, rows, span]
        dst = rbuf.at[c, mine, rows, span]
        stays = (off == 0) & (parity == c)

        @pl.when(jnp.logical_not(stays))
        def _():
            pltpu.make_async_remote_copy(
                src, dst, xy_send, sem, device_id=(chip(yy, z, xx), parity), device_id_type=MESH
            ).start()

        @pl.when(stays)
        def _():
            pltpu.make_async_copy(src, dst, sem).start()

    early_rows, late_rows = pl.ds(0, g.early), pl.ds(g.early, g.slots - g.early)

    def near_span(n):
        return g.starts[g.near[n][0]], sum(g.ahead[q] for q in g.near[n])

    def gather_near(n):
        start, width = near_span(n)
        rows = xall[:g.reach, :, start:start + width].reshape(g.reach * g.tok, width)
        got = nn(pick_near[...], rows).astype(BF16)
        sbuf[:, :g.early, start:start + width] = got.reshape(g.xy, g.early, width)

        @pl.loop(0, g.xy)
        def _(off):
            to_plane(early_rows, pl.ds(start, width), near_recv.at[c, n], off)

    def gather_far(q):
        start, width = g.starts[q], g.ahead[q]
        rows = xall[g.reach - 1:, :, start:start + width].reshape(g.col - (g.reach - 1) * g.tok, width)
        groups = 4
        per = g.xy // groups
        late = g.slots - g.early
        for i in range(groups):
            got = nn(pick_far[i * per * late:(i + 1) * per * late, :], rows).astype(BF16)
            sbuf[i * per:(i + 1) * per, g.early:, start:start + width] = got.reshape(per, late, width)

        @pl.loop(0, g.xy)
        def _(off):
            to_plane(late_rows, pl.ds(start, width), xy_recv.at[c, q], off)

    arrived = set()

    def need(q, steps):
        for at in steps:
            for way in range(2):
                if at <= hops(q, way) and (q, way, at) not in arrived:
                    arrived.add((q, way, at))
                    z_copy(q, way, at).wait_recv()

    def need_one(q, way, at):
        if at and (q, way, at) not in arrived:
            arrived.add((q, way, at))
            z_copy(q, way, at).wait_recv()

    swapped = False
    for step in ring_plan(g.ahead, g.near, g.nz // 2):
        if step[0] == "send":
            _, q, way, at = step
            need_one(q, way, at - 1)
            z_copy(q, way, at).start()
        elif step[0] == "tables":
            tables()
        elif step[0] == "tables_far":
            tables_far()
        elif step[0] == "near":
            for q in g.near[step[1]]:
                need(q, (1,))
            gather_near(step[1])
            if not swapped:
                swapped = True
                for i in range(3):
                    weight_own(i).wait()
                    weight_swap(i).start()
        else:
            need(step[1], range(1, g.nz // 2 + 1))
            gather_far(step[1])

    early = lax.broadcasted_iota(jnp.int32, (g.col, g.col), 0)
    late = lax.broadcasted_iota(jnp.int32, (g.col, g.col), 1)
    same = jnp.where(early == late, 1.0, 0.0).astype(BF16)
    pick_t[...] = nt(same, pick[...]).astype(BF16)
    whole = scaled[...].reshape(g.xy, g.slots, g.col)
    for ref, (low, high, first, last) in ((near_t, g.tiers[0]), (mid_t, g.tiers[1]), (far_t, g.tiers[2])):
        cols = (last - first) * g.tok
        rows = whole[:, low:high, first * g.tok:last * g.tok].reshape(g.xy * (high - low), cols)
        ref[...] = nt(same[:cols, :cols], rows).astype(BF16)

    for i in range(3):
        weight_swap(i).wait()

    for q in range(g.nq):
        feats = slice(g.starts[q], g.starts[q] + g.ahead[q])
        for n, group in enumerate(g.near):
            if q == group[0]:
                start, width = near_span(n)
                for kind in range(2):
                    came = rbuf.at[kind, :, early_rows, pl.ds(start, width)]
                    pltpu.make_async_copy(came, came, near_recv.at[kind, n]).wait()
        for kind in range(2):
            came = rbuf.at[kind, :, late_rows, lanes(q)]
            pltpu.make_async_copy(came, came, xy_recv.at[kind, q]).wait()
        rows = rbuf[0, :, :, feats].reshape(g.rows, g.ahead[q])
        grads = rbuf[1, :, :, feats].reshape(g.rows, g.ahead[q])
        if q == 0:
            gacc[...] = nn(rows, wg[feats, :])
            uacc[...] = nn(rows, wu[feats, :])
            hacc[...] = nt(grads, wd[:, feats])
        else:
            hacc[...] += nt(grads, wd[:, feats])
            gacc[...] += nn(rows, wg[feats, :])
            uacc[...] += nn(rows, wu[feats, :])

    for i in range(g.src):
        span = slice(i * g.slots, (i + 1) * g.slots)
        gate_pre, up_pre, grad_hidden = gacc[span, :], uacc[span, :], hacc[span, :]
        sigma = jax.nn.sigmoid(gate_pre)
        down = grad_hidden * (gate_pre * sigma)
        score = jnp.sum(down * up_pre, axis=1, keepdims=True)
        wide = jnp.broadcast_to(score, (g.slots, LANES)).astype(BF16)
        first = jnp.where(lax.broadcasted_iota(jnp.int32, (16, LANES), 1) == 0, 1.0, 0.0).astype(BF16)
        ret[0][0, i, :, :g.slots] = nt(first, wide).astype(BF16)
        gu[span, :] = down.astype(BF16)
        gg[span, :] = (grad_hidden * up_pre * sigma * (1.0 + gate_pre * (1.0 - sigma))).astype(BF16)

    here_d = y * g.nx + x

    def to_source(j, h, i, rows, sem):
        dy = i // (g.nx // 2)
        dx = 2 * lax.rem(i, g.nx // 2) + lax.rem(dy + parity + c, 2)
        yy = lax.rem(y + dy, g.ny)
        xx = lax.rem(x + dx, g.nx)
        src = ret[j].at[h if j else 0, yy * (g.nx // 2) + xx // 2, rows]
        dst = back[j].at[here_d, rows]
        stays = (xx == x) & (yy == y) & (c == h)

        @pl.when(jnp.logical_not(stays))
        def _():
            pltpu.make_async_remote_copy(
                src, dst, ret_send.at[j], sem, device_id=(chip(yy, z, xx), h), device_id_type=MESH
            ).start()

        @pl.when(stays)
        def _():
            pltpu.make_async_copy(src, dst, sem).start()

    def tier_rows(n):
        return pl.ds(g.tiers[n][0], g.tiers[n][1] - g.tiers[n][0])

    def send_back(j, rows, sem):
        @pl.loop(0, g.src)
        def _(i):
            for h in range(2):
                to_source(j, h, i, rows, sem)

    def make(j):
        w = g.widths[j]
        if j:
            cuts = [h * g.dh + g.cuts[j] for h in range(2)]
            both = [jnp.concatenate([ref[cut:cut + w, :] for cut in cuts], axis=0) for ref in (wg, wu)]
            got = (nt(gg[...], both[0]) + nt(gu[...], both[1])).astype(BF16)
            for h in range(2):
                ret[j][h] = got[:, h * w:(h + 1) * w].reshape(g.src, g.slots, w)

        send_back(j, tier_rows(2) if j else pl.ds(0, 16), ret_recv.at[j])

    def combine(j):
        came = back[j].at[:, tier_rows(2) if j else pl.ds(0, 16)]
        pltpu.make_async_copy(came, came, ret_recv.at[j]).wait()
        if j == 0:
            slot = lax.broadcasted_iota(jnp.int32, (g.slots, g.slots), 0)
            same = jnp.where(slot == lax.broadcasted_iota(jnp.int32, (g.slots, g.slots), 1), 1.0, 0.0).astype(BF16)
            at = lax.broadcasted_iota(jnp.int32, (g.slots, LANES), 1)
            placed = []
            for d in range(g.xy):
                column = nt(same, back[0][d, :, :g.slots])[:, :1]
                expert = ((d // g.nx) * g.nz + z) * g.nx + d % g.nx
                placed.append(jnp.where(at == expert, column, 0.0).astype(BF16))
            part[0][...] = nn(pick_t[...], jnp.concatenate(placed, axis=0))
        else:
            got, first, _ = tier_sum(j, far_t, 2)
            part[j][first * g.tok:, :] = got

    def tier_sum(j, weights, n):
        low, high, first, last = g.tiers[n]
        rows = back[j][:, low:high, :].reshape(g.xy * (high - low), g.widths[j])
        return nn(weights[...], rows), first, last

    def combine_more(j, weights, n, sem):
        came = back[j].at[:, tier_rows(n)]
        pltpu.make_async_copy(came, came, sem).wait()
        got, first, last = tier_sum(j, weights, n)
        edge = (last - 1 - first) * g.tok
        part[j][first * g.tok:(last - 1) * g.tok, :] = got[:edge]
        part[j][(last - 1) * g.tok:last * g.tok, :] += got[edge:]

    def own_part(j, away):
        block = g.at(away)
        return part[j][block * g.tok:(block + 1) * g.tok, :]

    def spot(j, way, step):
        return step - 1 + way * hops(j, 0)

    def rs_copy(j, way, step):
        sign = 1 - 2 * way
        n = spot(j, way, step)
        return pltpu.make_async_remote_copy(
            rsend[j].at[n], rrecv[j].at[n], rs_send.at[j], rs_recv.at[j, n],
            device_id=(chip(y, zmod(z + sign), x), c), device_id_type=MESH,
        )

    passed = {}

    def rs_next(j, way):
        n = hops(j, way)
        at = passed.get((j, way), 0) + 1
        passed[j, way] = at
        sign = 1 - 2 * way
        term = own_part(j, sign * (n + 1 - at))
        if at > 1:
            rs_copy(j, way, at - 1).wait_recv()
            term = term + rrecv[j][spot(j, way, at - 1)].astype(F32)
        rsend[j][spot(j, way, at)] = term.astype(BF16)
        rs_copy(j, way, at).start()

    def rs_move(j, kind):
        for way in range(2):
            n, done = hops(j, way), passed.get((j, way), 0)
            if j == 0:
                go = done < n
            elif kind == "combine":
                go = g.at((1 - 2 * way) * n) >= g.tiers[1][3]
            elif kind == "add":
                go = done < n - 1
            else:
                go = True
            if go:
                rs_next(j, way)

    def swap(j):
        span = pl.ds(pl.multiple_of(c * g.dh + g.cuts[j], LANES), g.widths[j])
        return pltpu.make_async_remote_copy(
            out_ref.at[:, span], out_ref.at[:, span], out_send, out_recv,
            device_id=(e, other), device_id_type=MESH,
        )

    def rs_last(j):
        total = own_part(j, 0)
        for way in range(2):
            rs_copy(j, way, hops(j, way)).wait_recv()
            total = total + rrecv[j][spot(j, way, hops(j, way))].astype(F32)
        if j:
            out_ref[:, pl.ds(pl.multiple_of(c * g.dh + g.cuts[j], LANES), g.widths[j])] = total.astype(BF16)
            swap(j).start()
        else:
            square = (LANES, LANES)
            same = lax.broadcasted_iota(jnp.int32, square, 0) == lax.broadcasted_iota(jnp.int32, square, 1)
            scores = nt(jnp.where(same, 1.0, 0.0).astype(BF16), total.astype(BF16))
            expert_at = lax.broadcasted_iota(jnp.int32, (LANES, g.tok), 0)
            for k in range(g.top):
                one = jnp.where(expert_at == ids_ref[k:k + 1, :], scores, 0.0)
                gate_ref[k:k + 1, :] = jnp.sum(one, axis=0, keepdims=True)

    for kind, j, *_ in sum_plan(g.widths, g.nz // 2):
        if kind == "make":
            make(j)
        elif kind == "middle":
            send_back(j, tier_rows(1), mid_recv.at[j])
        elif kind == "near":
            send_back(j, tier_rows(0), back_recv.at[j])
        elif kind == "last":
            rs_last(j)
        else:
            if kind == "combine":
                combine(j)
            elif kind == "mid":
                combine_more(j, mid_t, 1, mid_recv.at[j])
            elif kind == "close":
                combine_more(j, near_t, 0, back_recv.at[j])
            rs_move(j, kind)

    def gone(ref, sem):
        pltpu.make_async_copy(ref, ref, sem).wait()

    some = pl.ds(0, g.nz - 1)
    gone(rawall.at[some], raw_send)
    gone(xall.at[some], z_send)
    for j in range(g.nj):
        gone(rsend[j], rs_send.at[j])

    @pl.when(parity == c)
    def _():
        fewer = pl.ds(0, g.xy - 1)
        gone(sbuf.at[fewer], xy_send)
        for j in range(g.nj):
            gone(back[j].at[fewer], ret_send.at[j])

    @pl.when(parity != c)
    def _():
        gone(sbuf, xy_send)
        for j in range(g.nj):
            gone(back[j], ret_send.at[j])

    half = out_ref.at[:, pl.ds(0, g.dh)]
    gone(half, out_send)
    gone(half, out_recv)


def scratch(g):
    dma = pltpu.SemaphoreType.DMA
    half = g.nz // 2
    vm = pltpu.VMEM
    return [
        vm((g.top, g.tok), jnp.int32),
        vm((g.top, g.tok), F32),
        vm((g.nz, g.tok, g.dim), BF16),
        vm((g.nz, 2 * g.top, LANES), F32),
        vm((g.xy * g.early, g.reach * g.tok), BF16),
        vm((g.xy * (g.slots - g.early), g.col - (g.reach - 1) * g.tok), BF16),
        vm((g.all_slots, g.col), BF16),
        vm((g.all_slots, g.col), BF16),
        vm((g.col, g.all_slots), BF16),
        *[vm(((last - first) * g.tok, g.xy * (high - low)), BF16) for low, high, first, last in g.tiers],
        vm((g.xy, g.slots, g.dim), BF16),
        vm((2, g.src, g.slots, g.dim), BF16),
        vm((g.dim, g.ff), BF16),
        vm((g.dim, g.ff), BF16),
        vm((g.ff, g.dim), BF16),
        vm((g.rows, g.ff), F32),
        vm((g.rows, g.ff), F32),
        vm((g.rows, g.ff), F32),
        vm((g.rows, g.ff), BF16),
        vm((g.rows, g.ff), BF16),
        dma((2,)),
        dma(()),
        dma((3,)),
        dma((3,)),
        dma((3,)),
        dma(()),
        dma((2,)),
        dma(()),
        dma((g.nq, 2, half)),
        dma(()),
        dma((2, len(g.near))),
        dma((2, g.nq)),
        dma((g.nj,)),
        dma((g.nj,)),
        dma((g.nj,)),
        dma((g.nj,)),
        dma((g.nj,)),
        dma((g.nj, g.nz - 1)),
        dma(()),
        dma(()),
        *[vm((2 if j else 1, g.src, g.slots if j else 16, w), BF16) for j, w in enumerate(g.widths)],
        *[vm((g.xy, g.slots if j else 16, w), BF16) for j, w in enumerate(g.widths)],
        *[vm((g.col, w), F32) for w in g.widths],
        *[vm((g.nz - 1, g.tok, w), BF16) for w in g.widths],
        *[vm((g.nz - 1, g.tok, w), BF16) for w in g.widths],
    ]


def per_device(ny, nz, nx, ahead, near, widths, tokens, cotangent, expert_ids, gate_weights, w_gate, w_up, w_down):
    tok, dim = tokens.shape
    top = expert_ids.shape[1]
    g = Sizes(tok, dim, w_gate.shape[2], top, ny, nz, nx, ahead, near, widths)
    vmem = pl.BlockSpec(memory_space=pltpu.VMEM)
    hbm = pl.BlockSpec(memory_space=pl.ANY)
    input_grad, gate_grad = pl.pallas_call(
        functools.partial(kernel, g),
        out_shape=(
            pltpu.VMEM((tok, dim), BF16),
            pltpu.VMEM((top, tok), F32),
        ),
        in_specs=[hbm] * 7,
        out_specs=(vmem, vmem),
        scratch_shapes=scratch(g),
        compiler_params=pltpu.CompilerParams(
            collective_id=0, has_side_effects=True, vmem_limit_bytes=60 * 1024 * 1024
        ),
    )(expert_ids.T, gate_weights.T, tokens, cotangent, w_gate, w_up, w_down)
    return input_grad, gate_grad.T.astype(BF16)


def solution(mesh, ny=NY, nz=NZ, nx=NX, ahead=(256,) * 8, near=((0,), (1,), (2,), (3,), (4, 5), (6, 7)), widths=(LANES, 256, 256, 256, 256)):
    placed = (
        P("expert", None),
        P("expert", None),
        P("expert", None),
        P("expert", None),
        P("expert", None, "half"),
        P("expert", None, "half"),
        P("expert", "half", None),
    )
    return jax.shard_map(
        functools.partial(per_device, ny, nz, nx, ahead, near, widths),
        mesh=mesh,
        in_specs=placed,
        out_specs=(P("expert", None), P("expert", None)),
        check_vma=False,
    )
```
